32 devices in a mesh: gz: 8 (over z, y), gy: 4 (over x, core).
Axes of the slice: x: 2, y: 2, z: 4, core: 2. Of those that a mesh axis runs over, the one named last changes fastest.
Arguments:
- phase: float32 [32, 128, 768], P('gz', 'gy'), may hold values from 0 to 1
- solute: float32 [32, 128, 768], P('gz', 'gy'), may hold values from -0.5 to 0.5
- labels: int32 [32, 128, 768], P('gz', 'gy'), may hold values from 0 to 31
- quat_table: float32 [32, 4], replicated, may hold values from -3 to 3
- heat_map: float32 [128, 768], P('gy'), may hold values from -4 to 4
- cotangent: float32 [6, 32, 128, 768], P(None, 'gz', 'gy'), may hold values from -6 to 6
Outputs:
- final_fields: float32 [6, 32, 128, 768], P(None, 'gz', 'gy')
- sensitivity: float32 [128, 768], P('gy')
- objective: float32 [], replicated
The draws below stay inside these ranges and needn't reach their ends.
All inputs are finite; a program needn't handle non-finite values.
Results may differ from the reference program's by a relative error of at most 0.0003.
Values sent between devices are 32-bit elements; how exact they have to be, the bound alone decides.
A program may use at most 128 MiB of HBM per device.

```python
import jax
import jax.numpy as jnp
from jax import lax

NX = 768
GRAINS = 32
NY = 128
NZ = 32


def touch_ends(drawn, key, least, high):
    longest = drawn.shape.index(max(drawn.shape))
    spots = []
    for shift in (0, 1):
        where = [jax.random.randint(jax.random.fold_in(key, axis), (), 0, length) for axis, length in enumerate(drawn.shape)]
        where[longest] = (where[longest] + shift) % drawn.shape[longest]
        spots.append(tuple(where))
    return drawn.at[spots[0]].set(least).at[spots[1]].set(high)


def block_levels(rng, shape, split, least, high):
    def one(position, blocks):
        heights = jax.random.uniform(jax.random.fold_in(jax.random.fold_in(rng, 6), position), (blocks,), jnp.float32, least / len(split), high / len(split))
        return jnp.repeat(jnp.exp(heights), shape[position] // blocks).reshape((-1,) + (1,) * (len(shape) - position - 1))

    loudness = one(*split[0])
    for cut in split[1:]:
        loudness = loudness * one(*cut)
    return loudness


def normal_values(own_key, extent, spread, reach, pieces=(), kind=jnp.bfloat16):
    array = spread * jax.random.normal(own_key, extent, jnp.float32)
    if pieces:
        array = array * block_levels(own_key, extent, pieces, -0.22, 0.18)
    return jnp.clip(array, -reach, reach).astype(kind)


def setup_inputs(seed: int = 0) -> dict:
    streams_of = jax.random.split(jax.random.key(seed), 7)
    phase = jnp.clip(1.0 * jax.random.uniform(streams_of[0], (NZ, NY, NX), jnp.float32) ** block_levels(streams_of[0], (NZ, NY, NX), ((0, 8), (1, 4)), -0.2, 0.2), 0.0, 1.0)
    solute = jnp.clip(jax.random.uniform(streams_of[1], (NZ, NY, NX), jnp.float32, -0.5, 0.5) * block_levels(streams_of[1], (NZ, NY, NX), ((0, 8), (1, 4)), -0.4, 0.0), -0.5, 0.5)
    labels = touch_ends(jax.random.randint(streams_of[2], (NZ, NY, NX), 0, GRAINS), jax.random.fold_in(streams_of[2], 1), 0, GRAINS - 1).astype(jnp.int32)
    quat_table = normal_values(streams_of[3], (GRAINS, 4), 0.5, 3.0, (), jnp.float32)
    heat_map = normal_values(streams_of[4], (NY, NX), 1.0, 4.0, ((0, 4),), jnp.float32)
    cotangent = normal_values(streams_of[5], (6, NZ, NY, NX), 1.0, 6.0, ((1, 8), (2, 4)), jnp.float32)
    return {"phase": phase, "solute": solute, "labels": labels, "quat_table": quat_table, "heat_map": heat_map, "cotangent": cotangent}


time_step = 0.08
drive_gain = 0.6
misfit_gain = 0.2
solute_diff = 0.8
reject_gain = 0.5
solute_shift = 0.5

def advance(padded, heat_rows):
    center = padded[:, 1:-1, 1:-1, :]
    border = jnp.zeros_like(center[..., :1])
    laplace = padded[:, 2:, 1:-1, :] + padded[:, :-2, 1:-1, :] + padded[:, 1:-1, 2:, :] + padded[:, 1:-1, :-2, :] + jnp.concatenate([center[..., 1:], border], -1) + jnp.concatenate([border, center[..., :-1]], -1) - 6.0 * center
    phase_now = center[0]
    quaternions = center[1:5]
    solute_now = center[5]
    undercool = heat_rows[None] - solute_shift * solute_now
    misfit = lax.optimization_barrier(jnp.sum(quaternions * laplace[1:5], axis=0))
    phase_next = phase_now + time_step * (laplace[0] + 4.0 * phase_now * (1.0 - phase_now) * (phase_now - 0.5 + drive_gain * jnp.tanh(undercool)) + misfit_gain * phase_now * misfit)
    quat_next = quaternions + time_step * ((1.0 - phase_now) ** 2 + 0.1) * laplace[1:5]
    solute_next = solute_now + time_step * solute_diff * laplace[5] + reject_gain * (phase_next - phase_now) * solute_now
    return jnp.concatenate([phase_next[None], quat_next, solute_next[None]], 0)

def surround(fields):
    wrapped = jnp.concatenate([fields[:, -1:], fields, fields[:, :1]], 1)
    return jnp.pad(wrapped, ((0, 0), (0, 0), (1, 1), (0, 0)))

def reference(phase, solute, labels, quat_table, heat_map, cotangent):
    quaternions = jnp.moveaxis(quat_table[labels], -1, 0)
    initial = jnp.concatenate([phase[None], quaternions, solute[None]], 0)

    def forward(heat):
        return advance(surround(advance(surround(initial), heat)), heat)
    final_fields, pullback = jax.vjp(forward, heat_map)
    sensitivity = pullback(cotangent)[0]
    objective = jnp.sum(cotangent * final_fields)
    return (final_fields, sensitivity, objective)
```

```python
import functools

import jax
import jax.numpy as jnp
from jax import lax
from jax.experimental import pallas as pl
from jax.experimental.pallas import tpu as pltpu
from jax.sharding import PartitionSpec as P

MESH = pl.DeviceIdType.MESH
F32 = jnp.float32


def kernel(
    n, m, depth, rows, cols, per,
    phase, solute, labels, quats, heat_in, cot,
    out, sens_out, obj_out,
    E, lab, M, G, GP, CQ, W0, heat, table, sbuf, rbuf, obuf, orbuf, red, fin,
    lsem, ysend, yrecv, zsend, zrecv, fsend, frecv, csend, crecv, r1s, r1r, os, orr, r2s, r2r,
):
    gz = lax.axis_index("gz")
    gy = lax.axis_index("gy")
    up = lax.rem(gz + 1, n)
    down = lax.rem(gz + n - 1, n)
    is_low = gy == 0
    is_high = gy == m - 1
    low = jnp.maximum(gy - 1, 0)
    high = jnp.minimum(gy + 1, m - 1)
    tiles = rows // 8
    lanes = cols // 128
    D = depth
    own = pl.ds(8, rows)
    top = 8 + rows

    bar = pltpu.get_barrier_semaphore()
    for d in range(1, n):
        pl.semaphore_signal(bar, inc=1, device_id=(lax.rem(gz + d, n), gy), device_id_type=MESH)
    for d in range(1, m):
        pl.semaphore_signal(bar, inc=1, device_id=(gz, lax.rem(gy + d, m)), device_id_type=MESH)

    local = []
    dests = ((phase, E.at[0]), (solute, E.at[5]), (labels, lab))
    for k, (src, dst) in enumerate(dests):
        local.append(pltpu.make_async_copy(src, dst.at[pl.ds(2, D), own], lsem.at[k]))
    local.append(pltpu.make_async_copy(cot.at[0], G.at[0, pl.ds(1, D), own], lsem.at[3]))
    local.append(pltpu.make_async_copy(cot.at[5], G.at[1, pl.ds(1, D), own], lsem.at[4]))
    local.append(pltpu.make_async_copy(cot.at[pl.ds(1, 4)], CQ, lsem.at[5]))
    local.append(pltpu.make_async_copy(heat_in, heat.at[own], lsem.at[6]))
    for copy in local:
        copy.start()

    pl.semaphore_wait(bar, n - 1 + m - 1)

    def remote(src, dst, ss, rs, z, y):
        return pltpu.make_async_remote_copy(
            src_ref=src, dst_ref=dst, send_sem=ss, recv_sem=rs, device_id=(z, y), device_id_type=MESH
        )

    zc = []
    for k, (src, dst) in enumerate(dests):
        zc.append(remote(src.at[D - 1], dst.at[1, own], zsend.at[2 * k], zrecv.at[2 * k], up, gy))
        zc.append(remote(src.at[0], dst.at[D + 2, own], zsend.at[2 * k + 1], zrecv.at[2 * k + 1], down, gy))

    def second(t):
        found = []
        a, b = pl.ds(pl.multiple_of(t * 8, 8), 8), pl.ds(pl.multiple_of(t * 8 + 8, 8), 8)
        for k, (src, dst) in enumerate(dests):
            found.append(remote(src.at[D - 2, a], dst.at[0, b], fsend.at[2 * k, t], frecv.at[2 * k, t], up, gy))
            found.append(
                remote(src.at[1, a], dst.at[D + 3, b], fsend.at[2 * k + 1, t], frecv.at[2 * k + 1, t], down, gy)
            )
        return found

    for copy in zc:
        copy.start()
    to_high, to_low = [], []
    faces = [(s, d.at[pl.ds(2, D)]) for s, d in dests]
    faces += [(cot.at[0], G.at[0, pl.ds(1, D)]), (cot.at[5], G.at[1, pl.ds(1, D)])]
    for k, (src, dst) in enumerate(faces):
        to_high.append(
            remote(src.at[:, pl.ds(rows - 8, 8)], dst.at[:, pl.ds(0, 8)], ysend.at[k], yrecv.at[k], gz, high)
        )
        to_low.append(
            remote(src.at[:, pl.ds(0, 8)], dst.at[:, pl.ds(top, 8)], ysend.at[6 + k], yrecv.at[6 + k], gz, low)
        )
    to_high.append(
        remote(heat_in.at[pl.ds(rows - 8, 8)], heat.at[pl.ds(0, 8)], ysend.at[5], yrecv.at[5], gz, high)
    )
    to_low.append(remote(heat_in.at[pl.ds(0, 8)], heat.at[pl.ds(top, 8)], ysend.at[11], yrecv.at[11], gz, low))

    @pl.when(jnp.logical_not(is_high))
    def _():
        for copy in to_high:
            copy.start()

    @pl.when(jnp.logical_not(is_low))
    def _():
        for copy in to_low:
            copy.start()

    for t in range(tiles):
        for copy in second(t):
            copy.start()

    row = lax.broadcasted_iota(jnp.int32, (8, 128), 0)
    lane = lax.broadcasted_iota(jnp.int32, (8, 128), 1)
    zero = jnp.zeros((8, 128), F32)

    for k in range(4):
        entry = zero
        for grain in range(quats.shape[1]):
            entry = jnp.where(lane == grain, quats[k, grain], entry)
        table[k] = entry
    sbuf[...] = jnp.zeros_like(sbuf)
    obuf[...] = jnp.zeros_like(obuf)
    for z in (0, D + 1):
        G[1, z] = jnp.zeros((rows + 16, cols), F32)
        GP[z] = jnp.zeros((rows + 16, cols), F32)

    def ds8(t):
        return pl.ds(pl.multiple_of(t * 8, 8), 8)

    def expand(z, t):
        r = ds8(t)
        for j in range(lanes):
            x = pl.ds(j * 128, 128)
            ids = lab[z, r, x]
            for k in range(4):
                E[1 + k, z, r, x] = jnp.take_along_axis(table[k], ids, axis=1)

    def wipe(z, t):
        r = ds8(t)
        for k in range(6):
            E[k, z, r, :] = jnp.zeros((8, cols), F32)

    def loop(count, body):
        def step(i, carry):
            body(i)
            return carry

        lax.fori_loop(0, count, step, 0)

    def around(ref, lead, z, t, j, last):
        r, x = ds8(t), pl.ds(j * 128, 128)
        c = ref[(*lead, z, r, x)]
        before = ref[(*lead, z, ds8(jnp.maximum(t - 1, 0)), x)]
        after = ref[(*lead, z, ds8(jnp.minimum(t + 1, last)), x)]
        left = ref[(*lead, z, r, pl.ds((j - 1) * 128, 128))] if j else zero
        right = ref[(*lead, z, r, pl.ds((j + 1) * 128, 128))] if j < lanes - 1 else zero
        ys = pltpu.roll(jnp.where(row == 0, after, c), 7, 0) + pltpu.roll(jnp.where(row == 7, before, c), 1, 0)
        xs = pltpu.roll(jnp.where(lane == 0, right, c), 127, 1) + pltpu.roll(jnp.where(lane == 127, left, c), 1, 1)
        zs = ref[(*lead, z + 1, r, x)] + ref[(*lead, z - 1, r, x)]
        return c, zs + ys + xs - 6.0 * c

    def mid(z, t, inside):
        r = ds8(t)
        drop = ((t == 0) & is_low) | ((t == tiles + 1) & is_high)
        keep = jnp.where(drop, 0.0, 1.0)
        hr = ds8(t)
        for j in range(lanes):
            x = pl.ds(j * 128, 128)
            p, lp = around(E, (0,), z, t, j, tiles + 1)
            c, lc = around(E, (5,), z, t, j, tiles + 1)
            misfit = zero
            rate = 0.08 * ((1.0 - p) * (1.0 - p) + 0.1)
            for k in range(4):
                q, lq = around(E, (1 + k,), z, t, j, tiles + 1)
                misfit = misfit + q * lq
                M[1 + k, z - 1, r, x] = keep * (q + rate * lq)
            th = jnp.tanh(heat[hr, x] - 0.5 * c)
            pq = p * (1.0 - p)
            dp = 0.08 * (lp + 4.0 * pq * (p - 0.5 + 0.6 * th) + 0.2 * p * misfit)
            cn = keep * (c + 0.064 * lc + 0.5 * dp * c)
            M[0, z - 1, r, x] = keep * (p + dp)
            M[5, z - 1, r, x] = cn
            W0[z - 1, r, x] = 0.192 * pq * (1.0 - th * th)
            if inside:
                GP[z - 1, r, x] = G[0, z - 1, r, x] + 0.5 * cn * G[1, z - 1, r, x]

    def final(z, t, edge):
        zm = z - 1
        r = ds8(t)
        ro = ds8(t - 1)
        for j in range(lanes):
            x = pl.ds(j * 128, 128)
            p, lp = around(M, (0,), zm, t, j, tiles + 1)
            c, lc = around(M, (5,), zm, t, j, tiles + 1)
            gc, lgc = around(G, (1,), zm, t, j, tiles + 1)
            gp, lgp = around(GP, (), zm, t, j, tiles + 1)
            g0 = G[0, zm, r, x]
            rate = 0.08 * ((1.0 - p) * (1.0 - p) + 0.1)
            misfit, qterm, obj = zero, zero, zero
            for k in range(4):
                q, lq = around(M, (1 + k,), zm, t, j, tiles + 1)
                g = CQ[k, z - 2, ro, x]
                qn = q + rate * lq
                out[1 + k, z - 2, ro, x] = qn
                misfit = misfit + q * lq
                qterm = qterm + g * lq
                obj = obj + g * qn
            th = jnp.tanh(heat[r, x] - 0.5 * c)
            pq = p * (1.0 - p)
            drive = p - 0.5 + 0.6 * th
            dp = 0.08 * (lp + 4.0 * pq * drive + 0.2 * p * misfit)
            pn = p + dp
            cn = c + 0.064 * lc + 0.5 * dp * c
            out[0, z - 2, ro, x] = pn
            out[5, z - 2, ro, x] = cn
            obuf[...] += obj + g0 * pn + gc * cn
            w = 0.192 * pq * (1.0 - th * th)
            gw = gp * w
            lam_p = (
                gp * (1.0 + 0.08 * (4.0 * (1.0 - 2.0 * p) * drive + 4.0 * pq + 0.2 * misfit))
                + 0.08 * lgp
                - 0.5 * c * gc
                - 0.16 * (1.0 - p) * qterm
            )
            lam_c = gc * (1.0 + 0.5 * dp) + 0.064 * lgc - 0.5 * gw
            s = gw + (lam_p + 0.5 * E[5, z, r, x] * lam_c) * W0[zm, r, x]
            if edge is not None:
                s = s + W0[edge - 1, r, x] * (0.08 * gp + 0.032 * E[5, edge, r, x] * gc)
            b = (t - 1) * lanes + j
            sbuf[b] += s

    def grid(z0, zstep, t0, count, body):
        loop(2 * count, lambda i: body(z0 + zstep * (i // count), t0 + i % count))

    for copy in local[:3]:
        copy.wait()
    loop(D * tiles, lambda i: expand(2 + i // tiles, 1 + i % tiles))

    @pl.when(jnp.logical_not(is_low))
    def _():
        for copy in to_high:
            copy.wait_recv()
        loop(D, lambda i: expand(2 + i, 0))

    @pl.when(is_low)
    def _():
        loop(D + 2, lambda i: wipe(1 + i, 0))
        heat[pl.ds(0, 8), :] = jnp.zeros((8, cols), F32)
        for k in range(2):
            for z in range(D):
                G[k, 1 + z, pl.ds(0, 8), :] = jnp.zeros((8, cols), F32)

    @pl.when(jnp.logical_not(is_high))
    def _():
        for copy in to_low:
            copy.wait_recv()
        loop(D, lambda i: expand(2 + i, tiles + 1))

    @pl.when(is_high)
    def _():
        loop(D + 2, lambda i: wipe(1 + i, tiles + 1))
        heat[pl.ds(top, 8), :] = jnp.zeros((8, cols), F32)
        for k in range(2):
            for z in range(D):
                G[k, 1 + z, pl.ds(top, 8), :] = jnp.zeros((8, cols), F32)

    for copy in local[3:]:
        copy.wait()
    loop((D - 2) * (tiles + 2), lambda i: mid(3 + i // (tiles + 2), i % (tiles + 2), True))

    for copy in zc:
        copy.wait_recv()
    c_high, c_low = [], []
    i = 0
    for z in (1, D + 2):
        for _, dst in dests:
            c_high.append(
                remote(dst.at[z, pl.ds(rows, 8)], dst.at[z, pl.ds(0, 8)], csend.at[i], crecv.at[i], gz, high)
            )
            c_low.append(
                remote(dst.at[z, pl.ds(8, 8)], dst.at[z, pl.ds(top, 8)], csend.at[6 + i], crecv.at[6 + i], gz, low)
            )
            i += 1

    @pl.when(jnp.logical_not(is_high))
    def _():
        for copy in c_high:
            copy.start()

    @pl.when(jnp.logical_not(is_low))
    def _():
        for copy in c_low:
            copy.start()

    grid(1, D + 1, 1, tiles, expand)

    @pl.when(jnp.logical_not(is_low))
    def _():
        for copy in c_high:
            copy.wait_recv()
        loop(2, lambda i: expand(1 + (D + 1) * i, 0))

    @pl.when(jnp.logical_not(is_high))
    def _():
        for copy in c_low:
            copy.wait_recv()
        loop(2, lambda i: expand(1 + (D + 1) * i, tiles + 1))

    grid(2, D - 1, 0, tiles + 2, lambda z, t: mid(z, t, True))
    loop((D - 2) * tiles, lambda i: final(3 + i // tiles, 1 + i % tiles, None))

    def give(o):
        return remote(sbuf.at[pl.ds(o * per, per)], rbuf.at[gz], r1s.at[o], r1r.at[gz], o, gy)

    def take(o):
        return remote(sbuf.at[pl.ds(o * per, per)], rbuf.at[o], r1s.at[o], r1r.at[o], o, gy)

    def others(body):
        for o in range(n):

            @pl.when(gz != o)
            def _():
                body(o)

    given = 0
    for t in range(tiles):
        for copy in second(t):
            copy.wait_recv()

        def layers(i, t=t):
            z = 1 + (D + 1) * i
            expand(z - 1 + 2 * i, t + 1)
            mid(z, t + 1, False)
            final(2 + (D - 1) * i, t + 1, z)

        loop(2, layers)
        ready = n if t == tiles - 1 else (t + 1) * lanes // per
        for o in range(given, ready):

            @pl.when(gz != o)
            def _():
                give(o).start()

        given = ready

    sends = []
    for d in range(1, m):
        sends.append(remote(obuf, orbuf.at[gy], os.at[d - 1], orr.at[d - 1], gz, lax.rem(gy + d, m)))
    for copy in sends:
        copy.start()
    orbuf[gy] = obuf[...]
    rbuf[gz] = jnp.zeros((per, 8, 128), F32)
    for copy in sends:
        copy.wait_recv()
    others(lambda o: take(o).wait_recv())
    acc = sbuf[pl.ds(gz * per, per)]
    for d in range(n):
        acc = acc + rbuf[d]
    red[pl.ds(0, per)] = acc
    total = orbuf[0]
    for d in range(1, m):
        total = total + orbuf[d]
    red[per] = total
    bcast = []
    for d in range(1, n):
        bcast.append(remote(red, fin.at[gz], r2s.at[d - 1], r2r.at[d - 1], lax.rem(gz + d, n), gy))
    for copy in bcast:
        copy.start()
    fin[gz] = red[...]
    for copy in bcast:
        copy.wait_recv()
    total = fin[0, per]
    for d in range(1, n):
        total = total + fin[d, per]
    obj_out[0, 0] = jnp.sum(total)
    for b in range(tiles * lanes):
        sens_out[pl.ds(b // lanes * 8, 8), pl.ds(b % lanes * 128, 128)] = fin[b // per, b % per]

    for copy in zc + sends + bcast:
        copy.wait_send()
    others(lambda o: give(o).wait_send())
    for t in range(tiles):
        for copy in second(t):
            copy.wait_send()

    @pl.when(jnp.logical_not(is_high))
    def _():
        for copy in to_high + c_high:
            copy.wait_send()

    @pl.when(jnp.logical_not(is_low))
    def _():
        for copy in to_low + c_low:
            copy.wait_send()


def store(fields, sens, fields_out, sens_out, sem):
    copies = [pltpu.make_async_copy(fields.at[k], fields_out.at[k], sem.at[k]) for k in range(6)]
    copies.append(pltpu.make_async_copy(sens, sens_out, sem.at[6]))
    for copy in copies:
        copy.start()
    for copy in copies:
        copy.wait()


def solution(mesh):
    n, m = mesh.shape["gz"], mesh.shape["gy"]

    def on_device(phase, solute, labels, quat_table, heat_map, cotangent):
        depth, rows, cols = phase.shape
        blocks = rows // 8 * (cols // 128)
        per = -(-blocks // n)
        tall = rows + 16
        vmem = pl.BlockSpec(memory_space=pltpu.VMEM)
        hbm = pl.BlockSpec(memory_space=pltpu.HBM)
        smem = pl.BlockSpec(memory_space=pltpu.SMEM)
        fine = pltpu.SemaphoreType.DMA((6, rows // 8))
        dma = lambda k: pltpu.SemaphoreType.DMA((k,))
        final, sens, obj = pl.pallas_call(
            functools.partial(kernel, n, m, depth, rows, cols, per),
            out_shape=(
                pltpu.VMEM((6, depth, rows, cols), F32),
                pltpu.VMEM((rows, cols), F32),
                jax.ShapeDtypeStruct((1, 1), F32),
            ),
            in_specs=[hbm, hbm, hbm, smem, hbm, hbm],
            out_specs=(vmem, vmem, smem),
            scratch_shapes=[
                pltpu.VMEM((6, depth + 4, tall, cols), F32),
                pltpu.VMEM((depth + 4, tall, cols), jnp.int32),
                pltpu.VMEM((6, depth + 2, tall, cols), F32),
                pltpu.VMEM((2, depth + 2, tall, cols), F32),
                pltpu.VMEM((depth + 2, tall, cols), F32),
                pltpu.VMEM((4, depth, rows, cols), F32),
                pltpu.VMEM((depth + 2, tall, cols), F32),
                pltpu.VMEM((tall, cols), F32),
                pltpu.VMEM((4, 8, 128), F32),
                pltpu.VMEM((n * per, 8, 128), F32),
                pltpu.VMEM((n, per, 8, 128), F32),
                pltpu.VMEM((8, 128), F32),
                pltpu.VMEM((m, 8, 128), F32),
                pltpu.VMEM((per + 1, 8, 128), F32),
                pltpu.VMEM((n, per + 1, 8, 128), F32),
                dma(7), dma(12), dma(12), dma(6), dma(6), fine, fine, dma(12), dma(12),
                dma(n), dma(n), dma(m - 1), dma(m - 1), dma(n - 1), dma(n - 1),
            ],
            compiler_params=pltpu.CompilerParams(
                collective_id=0, has_side_effects=True, vmem_limit_bytes=56 * 1024 * 1024
            ),
        )(phase, solute, labels, quat_table.T, heat_map, cotangent)
        final, sens = pl.pallas_call(
            store,
            out_shape=(
                jax.ShapeDtypeStruct((6, depth, rows, cols), F32),
                jax.ShapeDtypeStruct((rows, cols), F32),
            ),
            in_specs=[vmem, vmem],
            out_specs=(hbm, hbm),
            scratch_shapes=[dma(7)],
            compiler_params=pltpu.CompilerParams(vmem_limit_bytes=4 * 1024 * 1024),
        )(final, sens)
        return final, sens, obj[0, 0]

    return jax.shard_map(
        on_device,
        mesh=mesh,
        in_specs=(
            P("gz", "gy", None),
            P("gz", "gy", None),
            P("gz", "gy", None),
            P(),
            P("gy", None),
            P(None, "gz", "gy", None),
        ),
        out_specs=(P(None, "gz", "gy", None), P("gy", None), P()),
        check_vma=False,
    )
```

```python
import functools

import jax
import jax.numpy as jnp
from jax import lax
from jax.experimental import pallas as pl
from jax.experimental.pallas import tpu as pltpu
from jax.sharding import PartitionSpec as P

MESH = pl.DeviceIdType.MESH
F32 = jnp.float32


def kernel(
    n, m, depth, rows, cols, per,
    phase, solute, labels, quats, heat_in, cot,
    out, sens_out, obj_out,
    E, lab, M, G, GP, CQ, W0, Z2P, Z2L, Z2C, heat, table, sbuf, rbuf, obuf, osend, orecv, red, fin,
    lsem, ysend, yrecv, zsend, zrecv, dsend, drecv, fsend, frecv, csend, crecv, r1s, r1r, os, orr, r2s, r2r,
):
    gz = lax.axis_index("gz")
    gy = lax.axis_index("gy")
    zs = [lax.rem(gz + d, n) for d in range(n)]
    ys = [lax.rem(gy + d, m) for d in range(m)]
    up, down = zs[1], zs[n - 1]
    is_low = gy == 0
    is_high = gy == m - 1
    low = jnp.maximum(gy - 1, 0)
    high = jnp.minimum(gy + 1, m - 1)
    tiles = rows // 8
    lanes = cols // 128
    D = depth
    own = pl.ds(8, rows)
    top = 8 + rows
    others = [(a, b) for a in range(n) for b in range(m) if a or b]

    bar = pltpu.get_barrier_semaphore()
    for a, b in others:
        pl.semaphore_signal(bar, inc=1, device_id=(zs[a], ys[b]), device_id_type=MESH)

    local = []
    dests = ((labels, lab), (phase, E.at[0]), (solute, E.at[5]))
    for k, (src, dst) in enumerate(dests):
        local.append(pltpu.make_async_copy(src, dst.at[pl.ds(1, D), own], lsem.at[k]))
    local.append(pltpu.make_async_copy(cot.at[0], G.at[0, pl.ds(1, D), own], lsem.at[3]))
    local.append(pltpu.make_async_copy(cot.at[5], G.at[1, pl.ds(1, D), own], lsem.at[4]))
    local.append(pltpu.make_async_copy(cot.at[pl.ds(1, 4)], CQ, lsem.at[5]))
    local.append(pltpu.make_async_copy(heat_in, heat.at[own], lsem.at[6]))
    for copy in local:
        copy.start()

    def remote(src, dst, ss, rs, z, y):
        return pltpu.make_async_remote_copy(
            src_ref=src, dst_ref=dst, send_sem=ss, recv_sem=rs, device_id=(z, y), device_id_type=MESH
        )

    near = []
    for k, (src, dst) in enumerate(dests):
        near.append(remote(src.at[D - 1], dst.at[0, own], zsend.at[2 * k], zrecv.at[2 * k], up, gy))
        near.append(remote(src.at[0], dst.at[D + 1, own], zsend.at[2 * k + 1], zrecv.at[2 * k + 1], down, gy))
    to_high, to_low = [], []
    faces = [(s, d, 2) for s, d in dests] + [(cot.at[0], G.at[0], 1), (cot.at[5], G.at[1], 1)]
    inner = pl.ds(1, D)
    for k, (src, dst, w) in enumerate(faces):
        to_high.append(
            remote(
                src.at[:, pl.ds(rows - w, w)], dst.at[inner, pl.ds(8 - w, w)], ysend.at[k], yrecv.at[k], gz, high
            )
        )
        to_low.append(
            remote(src.at[:, pl.ds(0, w)], dst.at[inner, pl.ds(top, w)], ysend.at[6 + k], yrecv.at[6 + k], gz, low)
        )
    to_high.append(
        remote(heat_in.at[pl.ds(rows - 1, 1)], heat.at[pl.ds(7, 1)], ysend.at[5], yrecv.at[5], gz, high)
    )
    to_low.append(remote(heat_in.at[pl.ds(0, 1)], heat.at[pl.ds(top, 1)], ysend.at[11], yrecv.at[11], gz, low))
    first, last = pl.ds(0, 1), pl.ds(rows - 1, 1)
    before, after = pl.ds(7, 1), pl.ds(top, 1)
    diag_high, diag_low = [], []
    for k, (src, dst) in enumerate(dests):
        i = 2 * k
        diag_high.append(remote(src.at[D - 1, last], dst.at[0, before], dsend.at[i], drecv.at[i], up, high))
        diag_low.append(remote(src.at[D - 1, first], dst.at[0, after], dsend.at[6 + i], drecv.at[6 + i], up, low))
        i += 1
        diag_high.append(remote(src.at[0, last], dst.at[D + 1, before], dsend.at[i], drecv.at[i], down, high))
        diag_low.append(
            remote(src.at[0, first], dst.at[D + 1, after], dsend.at[6 + i], drecv.at[6 + i], down, low)
        )

    def second(t):
        found = []
        a = pl.ds(t * 8, 8)
        for k, (src, dst) in enumerate(((labels, Z2L), (phase, Z2P))):
            i = 2 * k
            found.append(remote(src.at[D - 2, a], dst.at[0, a], fsend.at[i, t], frecv.at[i, t], up, gy))
            found.append(remote(src.at[1, a], dst.at[1, a], fsend.at[i + 1, t], frecv.at[i + 1, t], down, gy))
        return found

    second = [second(t) for t in range(tiles)]
    third = [
        remote(solute.at[D - 2], Z2C.at[0], csend.at[0], crecv.at[0], up, gy),
        remote(solute.at[1], Z2C.at[1], csend.at[1], crecv.at[1], down, gy),
    ]

    def start(copies):
        for copy in copies:
            copy.start()

    def sent(copies):
        for copy in copies:
            copy.wait_send()

    def arrived(copies):
        for copy in copies:
            copy.wait_recv()

    pl.semaphore_wait(bar, n * m - 1)
    start(near)

    @pl.when(jnp.logical_not(is_high))
    def _():
        start(to_high + diag_high)

    @pl.when(jnp.logical_not(is_low))
    def _():
        start(to_low + diag_low)

    row = lax.broadcasted_iota(jnp.int32, (8, 128), 0)
    lane = lax.broadcasted_iota(jnp.int32, (8, 128), 1)
    zero = jnp.zeros((8, 128), F32)

    for k in range(4):
        entry = zero
        for grain in range(quats.shape[1]):
            entry = jnp.where(lane == grain, quats[k, grain], entry)
        table[k] = entry
    sbuf[...] = jnp.zeros_like(sbuf)
    obuf[...] = jnp.zeros_like(obuf)
    for z in (0, D + 1):
        G[1, z] = jnp.zeros((rows + 16, cols), F32)
        GP[z] = jnp.zeros((rows + 16, cols), F32)

    def ds8(t):
        return pl.ds(pl.multiple_of(t * 8, 8), 8)

    def expand(z, t):
        r = ds8(t)
        for j in range(lanes):
            x = pl.ds(j * 128, 128)
            ids = lab[z, r, x]
            for k in range(4):
                E[1 + k, z, r, x] = jnp.take_along_axis(table[k], ids, axis=1)

    def wipe(z, t):
        r = ds8(t)
        for k in range(6):
            E[k, z, r, :] = jnp.zeros((8, cols), F32)

    def loop(count, body):
        def step(i, carry):
            body(i)
            return carry

        lax.fori_loop(0, count, step, 0)

    def around(ref, lead, z, t, j, toward=None):
        r, x = ds8(t), pl.ds(j * 128, 128)
        c = ref[(*lead, z, r, x)]
        above = ref[(*lead, z, ds8(jnp.maximum(t - 1, 0)), x)]
        below = ref[(*lead, z, ds8(jnp.minimum(t + 1, tiles + 1)), x)]
        left = ref[(*lead, z, r, pl.ds((j - 1) * 128, 128))] if j else zero
        right = ref[(*lead, z, r, pl.ds((j + 1) * 128, 128))] if j < lanes - 1 else zero
        ysum = pltpu.roll(jnp.where(row == 0, below, c), 7, 0) + pltpu.roll(jnp.where(row == 7, above, c), 1, 0)
        xsum = pltpu.roll(jnp.where(lane == 0, right, c), 127, 1) + pltpu.roll(jnp.where(lane == 127, left, c), 1, 1)
        if toward is None:
            zsum = ref[(*lead, z + 1, r, x)] + ref[(*lead, z - 1, r, x)]
        else:
            zsum = ref[(*lead, z + toward, r, x)]
        return c, zsum + ysum + xsum - 6.0 * c

    def keeping(t):
        drop = ((t == 0) & is_low) | ((t == tiles + 1) & is_high)
        return jnp.where(drop, 0.0, 1.0)

    def mid(z, t, inside, toward=None):
        r = ds8(t)
        keep = keeping(t)
        for j in range(lanes):
            x = pl.ds(j * 128, 128)
            p, lp = around(E, (0,), z, t, j, toward)
            c, lc = around(E, (5,), z, t, j, toward)
            misfit = zero
            rate = 0.08 * ((1.0 - p) * (1.0 - p) + 0.1)
            for k in range(4):
                q, lq = around(E, (1 + k,), z, t, j, toward)
                misfit = misfit + q * lq
                M[1 + k, z, r, x] = keep * (q + rate * lq)
            th = jnp.tanh(heat[r, x] - 0.5 * c)
            pq = p * (1.0 - p)
            dp = 0.08 * (lp + 4.0 * pq * (p - 0.5 + 0.6 * th) + 0.2 * p * misfit)
            cn = keep * (c + 0.064 * lc + 0.5 * dp * c)
            M[0, z, r, x] = keep * (p + dp)
            M[5, z, r, x] = cn
            W0[z, r, x] = 0.192 * pq * (1.0 - th * th)
            if inside:
                GP[z, r, x] = G[0, z, r, x] + 0.5 * cn * G[1, z, r, x]

    def bump(z, t, other):
        r = ds8(t)
        keep = keeping(t)
        for j in range(lanes):
            x = pl.ds(j * 128, 128)
            p = E[0, z, r, x]
            rate = keep * (0.08 * ((1.0 - p) * (1.0 - p) + 0.1))
            misfit = zero
            for k in range(4):
                q = E[1 + k, other, r, x]
                misfit = misfit + E[1 + k, z, r, x] * q
                M[1 + k, z, r, x] += rate * q
            dp = 0.08 * (E[0, other, r, x] + 0.2 * p * misfit)
            dc = keep * (0.064 * E[5, other, r, x] + 0.5 * dp * E[5, z, r, x])
            M[0, z, r, x] += keep * dp
            M[5, z, r, x] += dc
            GP[z, r, x] += 0.5 * dc * G[1, z, r, x]

    def bump_far(z, t, side):
        r, ro = ds8(t), ds8(t - 1)
        for j in range(lanes):
            x = pl.ds(j * 128, 128)
            p = E[0, z, r, x]
            rate = 0.08 * ((1.0 - p) * (1.0 - p) + 0.1)
            misfit = zero
            ids = Z2L[side, ro, x]
            for k in range(4):
                q = jnp.take_along_axis(table[k], ids, axis=1)
                misfit = misfit + E[1 + k, z, r, x] * q
                M[1 + k, z, r, x] += rate * q
            dp = 0.08 * (Z2P[side, ro, x] + 0.2 * p * misfit)
            M[0, z, r, x] += dp
            M[5, z, r, x] += 0.5 * dp * E[5, z, r, x]

    def final(z, t, edge):
        r = ds8(t)
        ro = ds8(t - 1)
        objective = zero
        for j in range(lanes):
            x = pl.ds(j * 128, 128)
            p, lp = around(M, (0,), z, t, j)
            c, lc = around(M, (5,), z, t, j)
            gc, lgc = around(G, (1,), z, t, j)
            gp, lgp = around(GP, (), z, t, j)
            g0 = G[0, z, r, x]
            rate = 0.08 * ((1.0 - p) * (1.0 - p) + 0.1)
            misfit, qterm = zero, zero
            for k in range(4):
                q, lq = around(M, (1 + k,), z, t, j)
                g = CQ[k, z - 1, ro, x]
                qn = q + rate * lq
                out[1 + k, z - 1, ro, x] = qn
                misfit = misfit + q * lq
                qterm = qterm + g * lq
                objective = objective + g * qn
            th = jnp.tanh(heat[r, x] - 0.5 * c)
            pq = p * (1.0 - p)
            drive = p - 0.5 + 0.6 * th
            dp = 0.08 * (lp + 4.0 * pq * drive + 0.2 * p * misfit)
            pn = p + dp
            cn = c + 0.064 * lc + 0.5 * dp * c
            out[0, z - 1, ro, x] = pn
            out[5, z - 1, ro, x] = cn
            objective = objective + g0 * pn + gc * cn
            w = 0.192 * pq * (1.0 - th * th)
            gw = gp * w
            lam_p = (
                gp * (1.0 + 0.08 * (4.0 * (1.0 - 2.0 * p) * drive + 4.0 * pq + 0.2 * misfit))
                + 0.08 * lgp
                - 0.5 * c * gc
                - 0.16 * (1.0 - p) * qterm
            )
            lam_c = gc * (1.0 + 0.5 * dp) + 0.064 * lgc - 0.5 * gw
            s = gw + (lam_p + 0.5 * E[5, z, r, x] * lam_c) * W0[z, r, x]
            if edge is not None:
                s = s + W0[edge, r, x] * (0.08 * gp + 0.032 * E[5, edge, r, x] * gc)
            sbuf[(t - 1) * lanes + j] += s
        obuf[...] += objective

    arrived_local = local[:3]
    for copy in arrived_local:
        copy.wait()
    loop(D * tiles, lambda i: expand(1 + i // tiles, 1 + i % tiles))

    @pl.when(jnp.logical_not(is_low))
    def _():
        arrived(to_high)
        loop(D, lambda i: expand(1 + i, 0))

    @pl.when(is_low)
    def _():
        loop(D + 2, lambda i: wipe(i, 0))
        heat[pl.ds(0, 8), :] = jnp.zeros((8, cols), F32)
        for k in range(2):
            for z in range(D):
                G[k, 1 + z, pl.ds(0, 8), :] = jnp.zeros((8, cols), F32)

    @pl.when(jnp.logical_not(is_high))
    def _():
        arrived(to_low)
        loop(D, lambda i: expand(1 + i, tiles + 1))

    @pl.when(is_high)
    def _():
        loop(D + 2, lambda i: wipe(i, tiles + 1))
        heat[pl.ds(top, 8), :] = jnp.zeros((8, cols), F32)
        for k in range(2):
            for z in range(D):
                G[k, 1 + z, pl.ds(top, 8), :] = jnp.zeros((8, cols), F32)

    for copy in local[3:]:
        copy.wait()
    tall = tiles + 2
    loop((D - 2) * tall, lambda i: mid(2 + i // tall, i % tall, True))
    loop(2 * tall, lambda i: mid(1 + (D - 1) * (i // tall), i % tall, True, 1 - 2 * (i // tall)))

    sent(near)
    for group in second:
        start(group)
    arrived(near)
    loop(2 * tiles, lambda i: expand((D + 1) * (i // tiles), 1 + i % tiles))

    @pl.when(jnp.logical_not(is_low))
    def _():
        arrived(diag_high)
        loop(2, lambda i: expand((D + 1) * i, 0))

    @pl.when(jnp.logical_not(is_high))
    def _():
        arrived(diag_low)
        loop(2, lambda i: expand((D + 1) * i, tiles + 1))

    loop(2 * tall, lambda i: bump(1 + (D - 1) * (i // tall), i % tall, (D + 1) * (i // tall)))
    loop(2 * tiles, lambda i: mid((D + 1) * (i // tiles), 1 + i % tiles, False, 1 - 2 * (i // tiles)))
    loop((D - 2) * tiles, lambda i: final(2 + i // tiles, 1 + i % tiles, None))

    def give(o):
        return remote(sbuf.at[pl.ds(o * per, per)], rbuf.at[gz], r1s.at[o], r1r.at[gz], o, gy)

    def take(o):
        return remote(sbuf.at[pl.ds(o * per, per)], rbuf.at[o], r1s.at[o], r1r.at[o], o, gy)

    def partners(action):
        for o in range(n):

            @pl.when(gz != o)
            def _():
                action(o)

    for group in second:
        sent(group)
    start(third)
    given = 0
    for t in range(tiles):
        arrived(second[t])

        def layers(i, t=t):
            bump_far((D + 1) * i, t + 1, i)
            final(1 + (D - 1) * i, t + 1, (D + 1) * i)

        loop(2, layers)
        ready = n if t == tiles - 1 else (t + 1) * lanes // per
        for o in range(given, ready):

            @pl.when(gz != o)
            def _():
                give(o).start()

        given = ready

    arrived(third)
    for side, z in ((0, 1), (1, D)):

        def correct(t, side=side, z=z):
            r, ro = ds8(t + 1), ds8(t)
            objective = zero
            for j in range(lanes):
                x = pl.ds(j * 128, 128)
                dc = 0.064 * 0.064 * Z2C[side, ro, x]
                out[5, z - 1, ro, x] += dc
                objective = objective + dc * G[1, z, r, x]
            obuf[...] += objective

        loop(tiles, correct)

    total = jnp.sum(obuf[...], axis=0, keepdims=True)
    osend[...] = total
    orecv[pl.ds(0, 1)] = total
    spread = []
    for a, b in others:
        i = a * m + b
        spread.append(remote(osend, orecv.at[pl.ds(i, 1)], os.at[i], orr.at[i], zs[a], ys[b]))
    start(spread)

    rbuf[gz] = sbuf[pl.ds(gz * per, per)]
    partners(lambda o: take(o).wait_recv())
    acc = rbuf[0]
    for d in range(1, n):
        acc = acc + rbuf[d]
    red[...] = acc
    bcast = []
    for d in range(1, n):
        bcast.append(remote(red, fin.at[gz], r2s.at[d - 1], r2r.at[d - 1], zs[d], gy))
    start(bcast)
    fin[gz] = acc
    arrived(spread)
    obj_out[0, 0] = jnp.sum(orecv[...])
    arrived(bcast)
    for b in range(tiles * lanes):
        sens_out[pl.ds(b // lanes * 8, 8), pl.ds(b % lanes * 128, 128)] = fin[b // per, b % per]

    sent(third + bcast + spread)
    partners(lambda o: give(o).wait_send())

    @pl.when(jnp.logical_not(is_high))
    def _():
        sent(to_high + diag_high)

    @pl.when(jnp.logical_not(is_low))
    def _():
        sent(to_low + diag_low)


def store(fields, sens, fields_out, sens_out, sem):
    copies = [pltpu.make_async_copy(fields.at[k], fields_out.at[k], sem.at[k]) for k in range(6)]
    copies.append(pltpu.make_async_copy(sens, sens_out, sem.at[6]))
    for copy in copies:
        copy.start()
    for copy in copies:
        copy.wait()


def solution(mesh):
    n, m = mesh.shape["gz"], mesh.shape["gy"]

    def on_device(phase, solute, labels, quat_table, heat_map, cotangent):
        depth, rows, cols = phase.shape
        blocks = rows // 8 * (cols // 128)
        per = -(-blocks // n)
        tall = rows + 16
        vmem = pl.BlockSpec(memory_space=pltpu.VMEM)
        hbm = pl.BlockSpec(memory_space=pltpu.HBM)
        smem = pl.BlockSpec(memory_space=pltpu.SMEM)
        fine = pltpu.SemaphoreType.DMA((4, rows // 8))
        dma = lambda k: pltpu.SemaphoreType.DMA((k,))
        final, sens, obj = pl.pallas_call(
            functools.partial(kernel, n, m, depth, rows, cols, per),
            out_shape=(
                pltpu.VMEM((6, depth, rows, cols), F32),
                pltpu.VMEM((rows, cols), F32),
                jax.ShapeDtypeStruct((1, 1), F32),
            ),
            in_specs=[hbm, hbm, hbm, smem, hbm, hbm],
            out_specs=(vmem, vmem, smem),
            scratch_shapes=[
                pltpu.VMEM((6, depth + 2, tall, cols), F32),
                pltpu.VMEM((depth + 2, tall, cols), jnp.int32),
                pltpu.VMEM((6, depth + 2, tall, cols), F32),
                pltpu.VMEM((2, depth + 2, tall, cols), F32),
                pltpu.VMEM((depth + 2, tall, cols), F32),
                pltpu.VMEM((4, depth, rows, cols), F32),
                pltpu.VMEM((depth + 2, tall, cols), F32),
                pltpu.VMEM((2, rows, cols), F32),
                pltpu.VMEM((2, rows, cols), jnp.int32),
                pltpu.VMEM((2, rows, cols), F32),
                pltpu.VMEM((tall, cols), F32),
                pltpu.VMEM((4, 8, 128), F32),
                pltpu.VMEM((n * per, 8, 128), F32),
                pltpu.VMEM((n, per, 8, 128), F32),
                pltpu.VMEM((8, 128), F32),
                pltpu.VMEM((1, 128), F32),
                pltpu.VMEM((n * m, 128), F32),
                pltpu.VMEM((per, 8, 128), F32),
                pltpu.VMEM((n, per, 8, 128), F32),
                dma(7), dma(12), dma(12), dma(6), dma(6), dma(12), dma(12), fine, fine, dma(2), dma(2),
                dma(n), dma(n), dma(n * m), dma(n * m), dma(n - 1), dma(n - 1),
            ],
            compiler_params=pltpu.CompilerParams(
                collective_id=0, has_side_effects=True, vmem_limit_bytes=56 * 1024 * 1024
            ),
        )(phase, solute, labels, quat_table.T, heat_map, cotangent)
        final, sens = pl.pallas_call(
            store,
            out_shape=(
                jax.ShapeDtypeStruct((6, depth, rows, cols), F32),
                jax.ShapeDtypeStruct((rows, cols), F32),
            ),
            in_specs=[vmem, vmem],
            out_specs=(hbm, hbm),
            scratch_shapes=[dma(7)],
            compiler_params=pltpu.CompilerParams(vmem_limit_bytes=4 * 1024 * 1024),
        )(final, sens)
        return final, sens, obj[0, 0]

    return jax.shard_map(
        on_device,
        mesh=mesh,
        in_specs=(
            P("gz", "gy", None),
            P("gz", "gy", None),
            P("gz", "gy", None),
            P(),
            P("gy", None),
            P(None, "gz", "gy", None),
        ),
        out_specs=(P(None, "gz", "gy", None), P("gy", None), P()),
        check_vma=False,
    )
```

```python
import functools

import jax
import jax.numpy as jnp
from jax import lax
from jax.experimental import pallas as pl
from jax.experimental.pallas import tpu as pltpu
from jax.sharding import PartitionSpec as P

MESH = pl.DeviceIdType.MESH
F32 = jnp.float32


def kernel(
    n, m, depth, rows, cols, per,
    phase, solute, labels, quats, heat_in, cot,
    out, sens_out, obj_out,
    E, lab, M, G, GP, CQ, W0, Z2P, Z2L, Z2C, heat, table, sbuf, rbuf, obuf, osend, orecv, red, fin,
    lsem, ysend, yrecv, zsend, zrecv, dsend, drecv, fsend, frecv, csend, crecv, r1s, r1r, os, orr, r2s, r2r,
):
    gz = lax.axis_index("gz")
    gy = lax.axis_index("gy")
    zs = [lax.rem(gz + d, n) for d in range(n)]
    ys = [lax.rem(gy + d, m) for d in range(m)]
    up, down = zs[1], zs[n - 1]
    is_low = gy == 0
    is_high = gy == m - 1
    low = jnp.maximum(gy - 1, 0)
    high = jnp.minimum(gy + 1, m - 1)
    tiles = rows // 8
    lanes = cols // 128
    D = depth
    own = pl.ds(8, rows)
    top = 8 + rows
    others = [(a, b) for a in range(n) for b in range(m) if a or b]

    bar = pltpu.get_barrier_semaphore()
    for a, b in others:
        pl.semaphore_signal(bar, inc=1, device_id=(zs[a], ys[b]), device_id_type=MESH)

    local = []
    dests = ((labels, lab), (phase, E.at[0]), (solute, E.at[5]))
    for k, (src, dst) in enumerate(dests):
        local.append(pltpu.make_async_copy(src, dst.at[pl.ds(1, D), own], lsem.at[k]))
    local.append(pltpu.make_async_copy(cot.at[0], G.at[0, pl.ds(1, D), own], lsem.at[3]))
    local.append(pltpu.make_async_copy(cot.at[5], G.at[1, pl.ds(1, D), own], lsem.at[4]))
    local.append(pltpu.make_async_copy(cot.at[pl.ds(1, 4)], CQ, lsem.at[5]))
    local.append(pltpu.make_async_copy(heat_in, heat.at[own], lsem.at[6]))
    for copy in local:
        copy.start()

    def remote(src, dst, ss, rs, z, y):
        return pltpu.make_async_remote_copy(
            src_ref=src, dst_ref=dst, send_sem=ss, recv_sem=rs, device_id=(z, y), device_id_type=MESH
        )

    odd = lax.rem(gz, 2)
    halo = ((D + 1) * (1 - odd), (D + 1) * odd)
    edge = (1 + (D - 1) * (1 - odd), 1 + (D - 1) * odd)
    into = (halo[1], halo[0])
    mate = (jnp.where(odd == 0, up, down), jnp.where(odd == 0, down, up))
    outer = (edge[0] - 1, edge[1] - 1)
    deeper = (1 + (D - 3) * (1 - odd), 1 + (D - 3) * odd)

    def nearest(w):
        return [
            remote(src.at[outer[w]], dst.at[into[w], own], zsend.at[2 * k + w], zrecv.at[2 * k + w], mate[w], gy)
            for k, (src, dst) in enumerate(dests)
        ]

    near = (nearest(0), nearest(1))
    to_high, to_low = [], []
    faces = [(s, d, 2) for s, d in dests] + [(cot.at[0], G.at[0], 1), (cot.at[5], G.at[1], 1)]
    inner = pl.ds(1, D)
    for k, (src, dst, w) in enumerate(faces):
        to_high.append(
            remote(
                src.at[:, pl.ds(rows - w, w)], dst.at[inner, pl.ds(8 - w, w)], ysend.at[k], yrecv.at[k], gz, high
            )
        )
        to_low.append(
            remote(src.at[:, pl.ds(0, w)], dst.at[inner, pl.ds(top, w)], ysend.at[6 + k], yrecv.at[6 + k], gz, low)
        )
    to_high.append(
        remote(heat_in.at[pl.ds(rows - 1, 1)], heat.at[pl.ds(7, 1)], ysend.at[5], yrecv.at[5], gz, high)
    )
    to_low.append(remote(heat_in.at[pl.ds(0, 1)], heat.at[pl.ds(top, 1)], ysend.at[11], yrecv.at[11], gz, low))
    first, last = pl.ds(0, 1), pl.ds(rows - 1, 1)
    before, after = pl.ds(7, 1), pl.ds(top, 1)
    diag_high, diag_low = [], []
    for k, (src, dst) in enumerate(dests):
        i = 2 * k
        diag_high.append(remote(src.at[D - 1, last], dst.at[0, before], dsend.at[i], drecv.at[i], up, high))
        diag_low.append(remote(src.at[D - 1, first], dst.at[0, after], dsend.at[6 + i], drecv.at[6 + i], up, low))
        i += 1
        diag_high.append(remote(src.at[0, last], dst.at[D + 1, before], dsend.at[i], drecv.at[i], down, high))
        diag_low.append(
            remote(src.at[0, first], dst.at[D + 1, after], dsend.at[6 + i], drecv.at[6 + i], down, low)
        )

    def distant(w):
        found = []
        for t in range(tiles):
            a = pl.ds(t * 8, 8)
            found.append([
                remote(src.at[deeper[w], a], dst.at[w, a], fsend.at[2 * k + w, t], frecv.at[2 * k + w, t], mate[w], gy)
                for k, (src, dst) in enumerate(((labels, Z2L), (phase, Z2P)))
            ])
        return found

    second = (distant(0), distant(1))
    third = [
        remote(solute.at[deeper[w]], Z2C.at[w], csend.at[w], crecv.at[w], mate[w], gy) for w in range(2)
    ]

    def start(copies):
        for copy in copies:
            copy.start()

    def sent(copies):
        for copy in copies:
            copy.wait_send()

    def arrived(copies):
        for copy in copies:
            copy.wait_recv()

    pl.semaphore_wait(bar, n * m - 1)
    @pl.when(jnp.logical_not(is_high))
    def _():
        start(diag_high + to_high)

    @pl.when(jnp.logical_not(is_low))
    def _():
        start(diag_low + to_low)

    start(near[1])

    start(near[0])

    for w in (1, 0):
        for group in second[w]:
            start(group)

    row = lax.broadcasted_iota(jnp.int32, (8, 128), 0)
    lane = lax.broadcasted_iota(jnp.int32, (8, 128), 1)
    zero = jnp.zeros((8, 128), F32)

    for k in range(4):
        entry = zero
        for grain in range(quats.shape[1]):
            entry = jnp.where(lane == grain, quats[k, grain], entry)
        table[k] = entry
    sbuf[...] = jnp.zeros_like(sbuf)
    obuf[...] = jnp.zeros_like(obuf)
    for z in (0, D + 1):
        G[1, z] = jnp.zeros((rows + 16, cols), F32)
        GP[z] = jnp.zeros((rows + 16, cols), F32)

    def ds8(t):
        return pl.ds(pl.multiple_of(t * 8, 8), 8)

    def expand(z, t):
        r = ds8(t)
        for j in range(lanes):
            x = pl.ds(j * 128, 128)
            ids = lab[z, r, x]
            for k in range(4):
                E[1 + k, z, r, x] = jnp.take_along_axis(table[k], ids, axis=1)

    def wipe(z, t):
        r = ds8(t)
        for k in range(6):
            E[k, z, r, :] = jnp.zeros((8, cols), F32)

    def loop(count, body):
        def step(i, carry):
            body(i)
            return carry

        lax.fori_loop(0, count, step, 0)

    def around(ref, lead, z, t, j, toward=None):
        r, x = ds8(t), pl.ds(j * 128, 128)
        c = ref[(*lead, z, r, x)]
        above = ref[(*lead, z, ds8(jnp.maximum(t - 1, 0)), x)]
        below = ref[(*lead, z, ds8(jnp.minimum(t + 1, tiles + 1)), x)]
        left = ref[(*lead, z, r, pl.ds((j - 1) * 128, 128))] if j else zero
        right = ref[(*lead, z, r, pl.ds((j + 1) * 128, 128))] if j < lanes - 1 else zero
        ysum = pltpu.roll(jnp.where(row == 0, below, c), 7, 0) + pltpu.roll(jnp.where(row == 7, above, c), 1, 0)
        xsum = pltpu.roll(jnp.where(lane == 0, right, c), 127, 1) + pltpu.roll(jnp.where(lane == 127, left, c), 1, 1)
        if toward is None:
            zsum = ref[(*lead, z + 1, r, x)] + ref[(*lead, z - 1, r, x)]
        else:
            zsum = ref[(*lead, z + toward, r, x)]
        return c, zsum + ysum + xsum - 6.0 * c

    def keeping(t):
        drop = ((t == 0) & is_low) | ((t == tiles + 1) & is_high)
        return jnp.where(drop, 0.0, 1.0)

    def mid(z, t, inside, toward=None):
        r = ds8(t)
        keep = keeping(t)
        for j in range(lanes):
            x = pl.ds(j * 128, 128)
            p, lp = around(E, (0,), z, t, j, toward)
            c, lc = around(E, (5,), z, t, j, toward)
            misfit = zero
            rate = 0.08 * ((1.0 - p) * (1.0 - p) + 0.1)
            for k in range(4):
                q, lq = around(E, (1 + k,), z, t, j, toward)
                misfit = misfit + q * lq
                M[1 + k, z, r, x] = keep * (q + rate * lq)
            th = jnp.tanh(heat[r, x] - 0.5 * c)
            pq = p * (1.0 - p)
            dp = 0.08 * (lp + 4.0 * pq * (p - 0.5 + 0.6 * th) + 0.2 * p * misfit)
            cn = keep * (c + 0.064 * lc + 0.5 * dp * c)
            M[0, z, r, x] = keep * (p + dp)
            M[5, z, r, x] = cn
            W0[z, r, x] = 0.192 * pq * (1.0 - th * th)
            if inside:
                GP[z, r, x] = G[0, z, r, x] + 0.5 * cn * G[1, z, r, x]

    def bump(z, t, other):
        r = ds8(t)
        keep = keeping(t)
        for j in range(lanes):
            x = pl.ds(j * 128, 128)
            p = E[0, z, r, x]
            rate = keep * (0.08 * ((1.0 - p) * (1.0 - p) + 0.1))
            misfit = zero
            for k in range(4):
                q = E[1 + k, other, r, x]
                misfit = misfit + E[1 + k, z, r, x] * q
                M[1 + k, z, r, x] += rate * q
            dp = 0.08 * (E[0, other, r, x] + 0.2 * p * misfit)
            dc = keep * (0.064 * E[5, other, r, x] + 0.5 * dp * E[5, z, r, x])
            M[0, z, r, x] += keep * dp
            M[5, z, r, x] += dc
            GP[z, r, x] += 0.5 * dc * G[1, z, r, x]

    def bump_far(z, t, side):
        r, ro = ds8(t), ds8(t - 1)
        for j in range(lanes):
            x = pl.ds(j * 128, 128)
            p = E[0, z, r, x]
            rate = 0.08 * ((1.0 - p) * (1.0 - p) + 0.1)
            misfit = zero
            ids = Z2L[side, ro, x]
            for k in range(4):
                q = jnp.take_along_axis(table[k], ids, axis=1)
                misfit = misfit + E[1 + k, z, r, x] * q
                M[1 + k, z, r, x] += rate * q
            dp = 0.08 * (Z2P[side, ro, x] + 0.2 * p * misfit)
            M[0, z, r, x] += dp
            M[5, z, r, x] += 0.5 * dp * E[5, z, r, x]

    def final(z, t, edge):
        r = ds8(t)
        ro = ds8(t - 1)
        objective = zero
        for j in range(lanes):
            x = pl.ds(j * 128, 128)
            p, lp = around(M, (0,), z, t, j)
            c, lc = around(M, (5,), z, t, j)
            gc, lgc = around(G, (1,), z, t, j)
            gp, lgp = around(GP, (), z, t, j)
            g0 = G[0, z, r, x]
            rate = 0.08 * ((1.0 - p) * (1.0 - p) + 0.1)
            misfit, qterm = zero, zero
            for k in range(4):
                q, lq = around(M, (1 + k,), z, t, j)
                g = CQ[k, z - 1, ro, x]
                qn = q + rate * lq
                out[1 + k, z - 1, ro, x] = qn
                misfit = misfit + q * lq
                qterm = qterm + g * lq
                objective = objective + g * qn
            th = jnp.tanh(heat[r, x] - 0.5 * c)
            pq = p * (1.0 - p)
            drive = p - 0.5 + 0.6 * th
            dp = 0.08 * (lp + 4.0 * pq * drive + 0.2 * p * misfit)
            pn = p + dp
            cn = c + 0.064 * lc + 0.5 * dp * c
            out[0, z - 1, ro, x] = pn
            out[5, z - 1, ro, x] = cn
            objective = objective + g0 * pn + gc * cn
            w = 0.192 * pq * (1.0 - th * th)
            gw = gp * w
            lam_p = (
                gp * (1.0 + 0.08 * (4.0 * (1.0 - 2.0 * p) * drive + 4.0 * pq + 0.2 * misfit))
                + 0.08 * lgp
                - 0.5 * c * gc
                - 0.16 * (1.0 - p) * qterm
            )
            lam_c = gc * (1.0 + 0.5 * dp) + 0.064 * lgc - 0.5 * gw
            s = gw + (lam_p + 0.5 * E[5, z, r, x] * lam_c) * W0[z, r, x]
            if edge is not None:
                s = s + W0[edge, r, x] * (0.08 * gp + 0.032 * E[5, edge, r, x] * gc)
            sbuf[(t - 1) * lanes + j] += s
        obuf[...] += objective

    arrived_local = local[:3]
    for copy in arrived_local:
        copy.wait()
    loop(D * tiles, lambda i: expand(1 + i // tiles, 1 + i % tiles))

    @pl.when(jnp.logical_not(is_low))
    def _():
        arrived(to_high)
        loop(D, lambda i: expand(1 + i, 0))

    @pl.when(is_low)
    def _():
        loop(D + 2, lambda i: wipe(i, 0))
        heat[pl.ds(0, 8), :] = jnp.zeros((8, cols), F32)
        for k in range(2):
            for z in range(D):
                G[k, 1 + z, pl.ds(0, 8), :] = jnp.zeros((8, cols), F32)

    @pl.when(jnp.logical_not(is_high))
    def _():
        arrived(to_low)
        loop(D, lambda i: expand(1 + i, tiles + 1))

    @pl.when(is_high)
    def _():
        loop(D + 2, lambda i: wipe(i, tiles + 1))
        heat[pl.ds(top, 8), :] = jnp.zeros((8, cols), F32)
        for k in range(2):
            for z in range(D):
                G[k, 1 + z, pl.ds(top, 8), :] = jnp.zeros((8, cols), F32)

    for copy in local[3:]:
        copy.wait()
    tall = tiles + 2
    loop((D - 2) * tall, lambda i: mid(2 + i // tall, i % tall, True))
    loop(2 * tall, lambda i: mid(1 + (D - 1) * (i // tall), i % tall, True, 1 - 2 * (i // tall)))

    @pl.when(jnp.logical_not(is_low))
    def _():
        arrived(diag_high)
        loop(2, lambda i: expand((D + 1) * i, 0))

    @pl.when(jnp.logical_not(is_high))
    def _():
        arrived(diag_low)
        loop(2, lambda i: expand((D + 1) * i, tiles + 1))

    def join(w):
        arrived(near[w])
        loop(tiles, lambda i: expand(halo[w], 1 + i))
        loop(tall, lambda i: bump(edge[w], i, halo[w]))
        loop(tiles, lambda i: mid(halo[w], 1 + i, False, edge[w] - halo[w]))

    step = halo[0] - edge[0]
    join(1)
    for t in range(tiles):
        arrived(second[1][t])
    loop(tiles, lambda i: bump_far(halo[1], 1 + i, 1))
    loop(tiles, lambda i: final(edge[1], 1 + i, halo[1]))
    loop((D - 3) * tiles, lambda i: final(edge[1] + step * (1 + i // tiles), 1 + i % tiles, None))
    join(0)
    loop(tiles, lambda i: final(edge[0] - step, 1 + i, None))

    def give(o):
        return remote(sbuf.at[pl.ds(o * per, per)], rbuf.at[gz], r1s.at[o], r1r.at[gz], o, gy)

    def take(o):
        return remote(sbuf.at[pl.ds(o * per, per)], rbuf.at[o], r1s.at[o], r1r.at[o], o, gy)

    def partners(action):
        for o in range(n):

            @pl.when(gz != o)
            def _():
                action(o)

    given = 0
    for t in range(tiles):
        arrived(second[0][t])
        if t == tiles - 2:
            start(third)
        bump_far(halo[0], t + 1, 0)
        final(edge[0], t + 1, halo[0])
        ready = n if t == tiles - 1 else (t + 1) * lanes // per
        for o in range(given, ready):

            @pl.when(gz != o)
            def _():
                give(o).start()

        given = ready

    for side in (1, 0):
        arrived([third[side]])

        def correct(t, side=side):
            r, ro = ds8(t + 1), ds8(t)
            objective = zero
            for j in range(lanes):
                x = pl.ds(j * 128, 128)
                dc = 0.064 * 0.064 * Z2C[side, ro, x]
                out[5, outer[side], ro, x] += dc
                objective = objective + dc * G[1, edge[side], r, x]
            obuf[...] += objective

        loop(tiles, correct)

    total = jnp.sum(obuf[...], axis=0, keepdims=True)
    osend[...] = total
    orecv[pl.ds(0, 1)] = total
    spread = []
    for a, b in others:
        i = a * m + b
        spread.append(remote(osend, orecv.at[pl.ds(i, 1)], os.at[i], orr.at[i], zs[a], ys[b]))
    start(spread)

    rbuf[gz] = sbuf[pl.ds(gz * per, per)]
    partners(lambda o: take(o).wait_recv())
    acc = rbuf[0]
    for d in range(1, n):
        acc = acc + rbuf[d]
    red[...] = acc
    bcast = []
    for d in range(1, n):
        bcast.append(remote(red, fin.at[gz], r2s.at[d - 1], r2r.at[d - 1], zs[d], gy))
    start(bcast)
    fin[gz] = acc
    arrived(spread)
    obj_out[0, 0] = jnp.sum(orecv[...])
    arrived(bcast)
    for b in range(tiles * lanes):
        sens_out[pl.ds(b // lanes * 8, 8), pl.ds(b % lanes * 128, 128)] = fin[b // per, b % per]

    sent(near[0] + near[1])
    for w in range(2):
        for group in second[w]:
            sent(group)
    sent(third + bcast + spread)
    partners(lambda o: give(o).wait_send())

    @pl.when(jnp.logical_not(is_high))
    def _():
        sent(to_high + diag_high)

    @pl.when(jnp.logical_not(is_low))
    def _():
        sent(to_low + diag_low)


def store(fields, sens, fields_out, sens_out, sem):
    copies = [pltpu.make_async_copy(fields.at[k], fields_out.at[k], sem.at[k]) for k in range(6)]
    copies.append(pltpu.make_async_copy(sens, sens_out, sem.at[6]))
    for copy in copies:
        copy.start()
    for copy in copies:
        copy.wait()


def solution(mesh):
    n, m = mesh.shape["gz"], mesh.shape["gy"]

    def on_device(phase, solute, labels, quat_table, heat_map, cotangent):
        depth, rows, cols = phase.shape
        blocks = rows // 8 * (cols // 128)
        per = -(-blocks // n)
        tall = rows + 16
        vmem = pl.BlockSpec(memory_space=pltpu.VMEM)
        hbm = pl.BlockSpec(memory_space=pltpu.HBM)
        smem = pl.BlockSpec(memory_space=pltpu.SMEM)
        fine = pltpu.SemaphoreType.DMA((4, rows // 8))
        dma = lambda k: pltpu.SemaphoreType.DMA((k,))
        final, sens, obj = pl.pallas_call(
            functools.partial(kernel, n, m, depth, rows, cols, per),
            out_shape=(
                pltpu.VMEM((6, depth, rows, cols), F32),
                pltpu.VMEM((rows, cols), F32),
                jax.ShapeDtypeStruct((1, 1), F32),
            ),
            in_specs=[hbm, hbm, hbm, smem, hbm, hbm],
            out_specs=(vmem, vmem, smem),
            scratch_shapes=[
                pltpu.VMEM((6, depth + 2, tall, cols), F32),
                pltpu.VMEM((depth + 2, tall, cols), jnp.int32),
                pltpu.VMEM((6, depth + 2, tall, cols), F32),
                pltpu.VMEM((2, depth + 2, tall, cols), F32),
                pltpu.VMEM((depth + 2, tall, cols), F32),
                pltpu.VMEM((4, depth, rows, cols), F32),
                pltpu.VMEM((depth + 2, tall, cols), F32),
                pltpu.VMEM((2, rows, cols), F32),
                pltpu.VMEM((2, rows, cols), jnp.int32),
                pltpu.VMEM((2, rows, cols), F32),
                pltpu.VMEM((tall, cols), F32),
                pltpu.VMEM((4, 8, 128), F32),
                pltpu.VMEM((n * per, 8, 128), F32),
                pltpu.VMEM((n, per, 8, 128), F32),
                pltpu.VMEM((8, 128), F32),
                pltpu.VMEM((1, 128), F32),
                pltpu.VMEM((n * m, 128), F32),
                pltpu.VMEM((per, 8, 128), F32),
                pltpu.VMEM((n, per, 8, 128), F32),
                dma(7), dma(12), dma(12), dma(6), dma(6), dma(12), dma(12), fine, fine, dma(2), dma(2),
                dma(n), dma(n), dma(n * m), dma(n * m), dma(n - 1), dma(n - 1),
            ],
            compiler_params=pltpu.CompilerParams(
                collective_id=0, has_side_effects=True, vmem_limit_bytes=56 * 1024 * 1024
            ),
        )(phase, solute, labels, quat_table.T, heat_map, cotangent)
        final, sens = pl.pallas_call(
            store,
            out_shape=(
                jax.ShapeDtypeStruct((6, depth, rows, cols), F32),
                jax.ShapeDtypeStruct((rows, cols), F32),
            ),
            in_specs=[vmem, vmem],
            out_specs=(hbm, hbm),
            scratch_shapes=[dma(7)],
            compiler_params=pltpu.CompilerParams(vmem_limit_bytes=4 * 1024 * 1024),
        )(final, sens)
        return final, sens, obj[0, 0]

    return jax.shard_map(
        on_device,
        mesh=mesh,
        in_specs=(
            P("gz", "gy", None),
            P("gz", "gy", None),
            P("gz", "gy", None),
            P(),
            P("gy", None),
            P(None, "gz", "gy", None),
        ),
        out_specs=(P(None, "gz", "gy", None), P("gy", None), P()),
        check_vma=False,
    )
```

```python
import functools

import jax
import jax.numpy as jnp
from jax import lax
from jax.experimental import pallas as pl
from jax.experimental.pallas import tpu as pltpu
from jax.sharding import PartitionSpec as P

MESH = pl.DeviceIdType.MESH
F32 = jnp.float32


def kernel(
    n, m, depth, rows, cols, per,
    phase, solute, labels, quats, heat_in, cot,
    out, sens_out, obj_out,
    E, lab, M, G, GP, CQ, W0, Z2P, Z2L, Z2C, heat, table, sbuf, rbuf, obuf, osend, orecv, red, fin,
    lsem, ysend, yrecv, zsend, zrecv, dsend, drecv, fsend, frecv, csend, crecv, r1s, r1r, os, orr, r2s, r2r,
):
    gz = lax.axis_index("gz")
    gy = lax.axis_index("gy")
    zs = [lax.rem(gz + d, n) for d in range(n)]
    ys = [lax.rem(gy + d, m) for d in range(m)]
    up, down = zs[1], zs[n - 1]
    is_low = gy == 0
    is_high = gy == m - 1
    low = jnp.maximum(gy - 1, 0)
    high = jnp.minimum(gy + 1, m - 1)
    tiles = rows // 8
    lanes = cols // 128
    D = depth
    own = pl.ds(8, rows)
    top = 8 + rows
    others = [(a, b) for a in range(n) for b in range(m) if a or b]

    bar = pltpu.get_barrier_semaphore()
    for a, b in others:
        pl.semaphore_signal(bar, inc=1, device_id=(zs[a], ys[b]), device_id_type=MESH)

    local = []
    dests = ((labels, lab), (phase, E.at[0]), (solute, E.at[5]))
    for k, (src, dst) in enumerate(dests):
        local.append(pltpu.make_async_copy(src, dst.at[pl.ds(1, D), own], lsem.at[k]))
    local.append(pltpu.make_async_copy(cot.at[0], G.at[0, pl.ds(1, D), own], lsem.at[3]))
    local.append(pltpu.make_async_copy(cot.at[5], G.at[1, pl.ds(1, D), own], lsem.at[4]))
    local.append(pltpu.make_async_copy(cot.at[pl.ds(1, 4)], CQ, lsem.at[5]))
    local.append(pltpu.make_async_copy(heat_in, heat.at[own], lsem.at[6]))
    for copy in local:
        copy.start()

    def remote(src, dst, ss, rs, z, y):
        return pltpu.make_async_remote_copy(
            src_ref=src, dst_ref=dst, send_sem=ss, recv_sem=rs, device_id=(z, y), device_id_type=MESH
        )

    odd = lax.rem(gz, 2)
    halo = ((D + 1) * (1 - odd), (D + 1) * odd)
    edge = (1 + (D - 1) * (1 - odd), 1 + (D - 1) * odd)
    into = (halo[1], halo[0])
    mate = (jnp.where(odd == 0, up, down), jnp.where(odd == 0, down, up))
    outer = (edge[0] - 1, edge[1] - 1)
    deeper = (1 + (D - 3) * (1 - odd), 1 + (D - 3) * odd)

    def nearest(w):
        return [
            remote(src.at[outer[w]], dst.at[into[w], own], zsend.at[2 * k + w], zrecv.at[2 * k + w], mate[w], gy)
            for k, (src, dst) in enumerate(dests)
        ]

    near = (nearest(0), nearest(1))
    to_high, to_low = [], []
    faces = [(s, d, 2) for s, d in dests] + [(cot.at[0], G.at[0], 1), (cot.at[5], G.at[1], 1)]
    inner = pl.ds(1, D)
    for k, (src, dst, w) in enumerate(faces):
        to_high.append(
            remote(
                src.at[:, pl.ds(rows - w, w)], dst.at[inner, pl.ds(8 - w, w)], ysend.at[k], yrecv.at[k], gz, high
            )
        )
        to_low.append(
            remote(src.at[:, pl.ds(0, w)], dst.at[inner, pl.ds(top, w)], ysend.at[6 + k], yrecv.at[6 + k], gz, low)
        )
    to_high.append(
        remote(heat_in.at[pl.ds(rows - 1, 1)], heat.at[pl.ds(7, 1)], ysend.at[5], yrecv.at[5], gz, high)
    )
    to_low.append(remote(heat_in.at[pl.ds(0, 1)], heat.at[pl.ds(top, 1)], ysend.at[11], yrecv.at[11], gz, low))
    first, last = pl.ds(0, 1), pl.ds(rows - 1, 1)
    before, after = pl.ds(7, 1), pl.ds(top, 1)
    diag_high, diag_low = [], []
    for k, (src, dst) in enumerate(dests):
        i = 2 * k
        diag_high.append(remote(src.at[D - 1, last], dst.at[0, before], dsend.at[i], drecv.at[i], up, high))
        diag_low.append(remote(src.at[D - 1, first], dst.at[0, after], dsend.at[6 + i], drecv.at[6 + i], up, low))
        i += 1
        diag_high.append(remote(src.at[0, last], dst.at[D + 1, before], dsend.at[i], drecv.at[i], down, high))
        diag_low.append(
            remote(src.at[0, first], dst.at[D + 1, after], dsend.at[6 + i], drecv.at[6 + i], down, low)
        )

    def distant(w):
        found = []
        for t in range(tiles):
            a = pl.ds(t * 8, 8)
            found.append([
                remote(src.at[deeper[w], a], dst.at[w, a], fsend.at[2 * k + w, t], frecv.at[2 * k + w, t], mate[w], gy)
                for k, (src, dst) in enumerate(((labels, Z2L), (phase, Z2P)))
            ])
        return found

    second = (distant(0), distant(1))
    third = [
        remote(solute.at[deeper[w]], Z2C.at[w], csend.at[w], crecv.at[w], mate[w], gy) for w in range(2)
    ]

    def start(copies):
        for copy in copies:
            copy.start()

    def sent(copies):
        for copy in copies:
            copy.wait_send()

    def arrived(copies):
        for copy in copies:
            copy.wait_recv()

    pl.semaphore_wait(bar, n * m - 1)
    @pl.when(jnp.logical_not(is_high))
    def _():
        start(diag_high + to_high)

    @pl.when(jnp.logical_not(is_low))
    def _():
        start(diag_low + to_low)

    start(near[1])

    start(near[0])

    for w in (1, 0):
        for group in second[w]:
            start(group)

    row = lax.broadcasted_iota(jnp.int32, (8, 128), 0)
    lane = lax.broadcasted_iota(jnp.int32, (8, 128), 1)
    zero = jnp.zeros((8, 128), F32)

    for k in range(4):
        entry = zero
        for grain in range(quats.shape[1]):
            entry = jnp.where(lane == grain, quats[k, grain], entry)
        table[k] = entry
    sbuf[...] = jnp.zeros_like(sbuf)
    obuf[...] = jnp.zeros_like(obuf)
    for z in (0, D + 1):
        G[1, z] = jnp.zeros((rows + 16, cols), F32)
        GP[z] = jnp.zeros((rows + 16, cols), F32)

    def ds8(t):
        return pl.ds(pl.multiple_of(t * 8, 8), 8)

    def expand(z, t):
        r = ds8(t)
        for j in range(lanes):
            x = pl.ds(j * 128, 128)
            ids = lab[z, r, x]
            for k in range(4):
                E[1 + k, z, r, x] = jnp.take_along_axis(table[k], ids, axis=1)

    def wipe(z, t):
        r = ds8(t)
        for k in range(6):
            E[k, z, r, :] = jnp.zeros((8, cols), F32)

    def loop(count, body):
        def step(i, carry):
            body(i)
            return carry

        lax.fori_loop(0, count, step, 0)

    def around(ref, lead, z, t, j, toward=None):
        r, x = ds8(t), pl.ds(j * 128, 128)
        c = ref[(*lead, z, r, x)]
        above = ref[(*lead, z, ds8(jnp.maximum(t - 1, 0)), x)]
        below = ref[(*lead, z, ds8(jnp.minimum(t + 1, tiles + 1)), x)]
        left = ref[(*lead, z, r, pl.ds((j - 1) * 128, 128))] if j else zero
        right = ref[(*lead, z, r, pl.ds((j + 1) * 128, 128))] if j < lanes - 1 else zero
        ysum = pltpu.roll(jnp.where(row == 0, below, c), 7, 0) + pltpu.roll(jnp.where(row == 7, above, c), 1, 0)
        xsum = pltpu.roll(jnp.where(lane == 0, right, c), 127, 1) + pltpu.roll(jnp.where(lane == 127, left, c), 1, 1)
        if toward is None:
            zsum = ref[(*lead, z + 1, r, x)] + ref[(*lead, z - 1, r, x)]
        else:
            zsum = ref[(*lead, z + toward, r, x)]
        return c, zsum + ysum + xsum - 6.0 * c

    def keeping(t):
        drop = ((t == 0) & is_low) | ((t == tiles + 1) & is_high)
        return jnp.where(drop, 0.0, 1.0)

    def mid(z, t, inside, toward=None):
        r = ds8(t)
        keep = keeping(t)
        for j in range(lanes):
            x = pl.ds(j * 128, 128)
            p, lp = around(E, (0,), z, t, j, toward)
            c, lc = around(E, (5,), z, t, j, toward)
            misfit = zero
            rate = 0.08 * ((1.0 - p) * (1.0 - p) + 0.1)
            for k in range(4):
                q, lq = around(E, (1 + k,), z, t, j, toward)
                misfit = misfit + q * lq
                M[1 + k, z, r, x] = keep * (q + rate * lq)
            th = jnp.tanh(heat[r, x] - 0.5 * c)
            pq = p * (1.0 - p)
            dp = 0.08 * (lp + 4.0 * pq * (p - 0.5 + 0.6 * th) + 0.2 * p * misfit)
            cn = keep * (c + 0.064 * lc + 0.5 * dp * c)
            M[0, z, r, x] = keep * (p + dp)
            M[5, z, r, x] = cn
            W0[z, r, x] = 0.192 * pq * (1.0 - th * th)
            if inside:
                GP[z, r, x] = G[0, z, r, x] + 0.5 * cn * G[1, z, r, x]

    def bump(z, t, other):
        r = ds8(t)
        keep = keeping(t)
        for j in range(lanes):
            x = pl.ds(j * 128, 128)
            p = E[0, z, r, x]
            rate = keep * (0.08 * ((1.0 - p) * (1.0 - p) + 0.1))
            misfit = zero
            for k in range(4):
                q = E[1 + k, other, r, x]
                misfit = misfit + E[1 + k, z, r, x] * q
                M[1 + k, z, r, x] += rate * q
            dp = 0.08 * (E[0, other, r, x] + 0.2 * p * misfit)
            dc = keep * (0.064 * E[5, other, r, x] + 0.5 * dp * E[5, z, r, x])
            M[0, z, r, x] += keep * dp
            M[5, z, r, x] += dc
            GP[z, r, x] += 0.5 * dc * G[1, z, r, x]

    def bump_far(z, t, side):
        r, ro = ds8(t), ds8(t - 1)
        for j in range(lanes):
            x = pl.ds(j * 128, 128)
            p = E[0, z, r, x]
            rate = 0.08 * ((1.0 - p) * (1.0 - p) + 0.1)
            misfit = zero
            ids = Z2L[side, ro, x]
            for k in range(4):
                q = jnp.take_along_axis(table[k], ids, axis=1)
                misfit = misfit + E[1 + k, z, r, x] * q
                M[1 + k, z, r, x] += rate * q
            dp = 0.08 * (Z2P[side, ro, x] + 0.2 * p * misfit)
            M[0, z, r, x] += dp
            M[5, z, r, x] += 0.5 * dp * E[5, z, r, x]

    def final(z, t, edge):
        r = ds8(t)
        ro = ds8(t - 1)
        objective = zero
        for j in range(lanes):
            x = pl.ds(j * 128, 128)
            p, lp = around(M, (0,), z, t, j)
            c, lc = around(M, (5,), z, t, j)
            gc, lgc = around(G, (1,), z, t, j)
            gp, lgp = around(GP, (), z, t, j)
            g0 = G[0, z, r, x]
            rate = 0.08 * ((1.0 - p) * (1.0 - p) + 0.1)
            misfit, qterm = zero, zero
            for k in range(4):
                q, lq = around(M, (1 + k,), z, t, j)
                g = CQ[k, z - 1, ro, x]
                qn = q + rate * lq
                out[1 + k, z - 1, ro, x] = qn
                misfit = misfit + q * lq
                qterm = qterm + g * lq
                objective = objective + g * qn
            th = jnp.tanh(heat[r, x] - 0.5 * c)
            pq = p * (1.0 - p)
            drive = p - 0.5 + 0.6 * th
            dp = 0.08 * (lp + 4.0 * pq * drive + 0.2 * p * misfit)
            pn = p + dp
            cn = c + 0.064 * lc + 0.5 * dp * c
            out[0, z - 1, ro, x] = pn
            out[5, z - 1, ro, x] = cn
            objective = objective + g0 * pn + gc * cn
            w = 0.192 * pq * (1.0 - th * th)
            gw = gp * w
            lam_p = (
                gp * (1.0 + 0.08 * (4.0 * (1.0 - 2.0 * p) * drive + 4.0 * pq + 0.2 * misfit))
                + 0.08 * lgp
                - 0.5 * c * gc
                - 0.16 * (1.0 - p) * qterm
            )
            lam_c = gc * (1.0 + 0.5 * dp) + 0.064 * lgc - 0.5 * gw
            s = gw + (lam_p + 0.5 * E[5, z, r, x] * lam_c) * W0[z, r, x]
            if edge is not None:
                s = s + W0[edge, r, x] * (0.08 * gp + 0.032 * E[5, edge, r, x] * gc)
            sbuf[(t - 1) * lanes + j] += s
        obuf[...] += objective

    arrived_local = local[:3]
    for copy in arrived_local:
        copy.wait()
    loop(D * tiles, lambda i: expand(1 + i // tiles, 1 + i % tiles))

    @pl.when(jnp.logical_not(is_low))
    def _():
        arrived(to_high)
        loop(D, lambda i: expand(1 + i, 0))

    @pl.when(is_low)
    def _():
        loop(D + 2, lambda i: wipe(i, 0))
        heat[pl.ds(0, 8), :] = jnp.zeros((8, cols), F32)
        for k in range(2):
            for z in range(D):
                G[k, 1 + z, pl.ds(0, 8), :] = jnp.zeros((8, cols), F32)

    @pl.when(jnp.logical_not(is_high))
    def _():
        arrived(to_low)
        loop(D, lambda i: expand(1 + i, tiles + 1))

    @pl.when(is_high)
    def _():
        loop(D + 2, lambda i: wipe(i, tiles + 1))
        heat[pl.ds(top, 8), :] = jnp.zeros((8, cols), F32)
        for k in range(2):
            for z in range(D):
                G[k, 1 + z, pl.ds(top, 8), :] = jnp.zeros((8, cols), F32)

    for copy in local[3:]:
        copy.wait()
    tall = tiles + 2
    loop((D - 2) * tall, lambda i: mid(2 + i // tall, i % tall, True))
    loop(2 * tall, lambda i: mid(1 + (D - 1) * (i // tall), i % tall, True, 1 - 2 * (i // tall)))

    @pl.when(jnp.logical_not(is_low))
    def _():
        arrived(diag_high)
        loop(2, lambda i: expand((D + 1) * i, 0))

    @pl.when(jnp.logical_not(is_high))
    def _():
        arrived(diag_low)
        loop(2, lambda i: expand((D + 1) * i, tiles + 1))

    def join(w):
        arrived(near[w])
        loop(tiles, lambda i: expand(halo[w], 1 + i))
        loop(tall, lambda i: bump(edge[w], i, halo[w]))
        loop(tiles, lambda i: mid(halo[w], 1 + i, False, edge[w] - halo[w]))

    step = halo[0] - edge[0]
    join(1)
    for t in range(tiles):
        arrived(second[1][t])
    loop(tiles, lambda i: bump_far(halo[1], 1 + i, 1))
    loop(tiles, lambda i: final(edge[1], 1 + i, halo[1]))
    loop((D - 3) * tiles, lambda i: final(edge[1] + step * (1 + i // tiles), 1 + i % tiles, None))
    join(0)
    loop(tiles, lambda i: final(edge[0] - step, 1 + i, None))

    mine = lax.rem(gz + n - n // 2 - 1, n)

    def owner(o):
        return (o + n // 2 + 1) % n

    def give(o):
        return remote(sbuf.at[pl.ds(o * per, per)], rbuf.at[gz], r1s.at[o], r1r.at[gz], owner(o), gy)

    def take(o):
        return remote(sbuf.at[pl.ds(o * per, per)], rbuf.at[o], r1s.at[o], r1r.at[o], o, gy)

    def partners(action):
        for o in range(n):

            @pl.when(gz != o)
            def _():
                action(o)

    given = 0
    for t in range(tiles):
        arrived(second[0][t])
        if t == tiles - 2:
            start(third)
        bump_far(halo[0], t + 1, 0)
        final(edge[0], t + 1, halo[0])
        ready = n if t == tiles - 1 else (t + 1) * lanes // per
        for o in range(given, ready):

            @pl.when(gz != owner(o))
            def _():
                give(o).start()

        given = ready

    for side in (1, 0):
        arrived([third[side]])

        def correct(t, side=side):
            r, ro = ds8(t + 1), ds8(t)
            objective = zero
            for j in range(lanes):
                x = pl.ds(j * 128, 128)
                dc = 0.064 * 0.064 * Z2C[side, ro, x]
                out[5, outer[side], ro, x] += dc
                objective = objective + dc * G[1, edge[side], r, x]
            obuf[...] += objective

        loop(tiles, correct)

    total = jnp.sum(obuf[...], axis=0, keepdims=True)
    osend[...] = total
    count = n * m - 1
    orecv[pl.ds(count, 1)] = total
    for i, (a, b) in enumerate(others):
        remote(osend, orecv.at[pl.ds(i, 1)], os.at[0], orr.at[0], zs[a], ys[b]).start()

    rbuf[gz] = sbuf[pl.ds(mine * per, per)]
    partners(lambda o: take(o).wait_recv())
    acc = rbuf[0]
    for d in range(1, n):
        acc = acc + rbuf[d]
    red[...] = acc
    bcast = []
    for d in range(1, n):
        bcast.append(remote(red, fin.at[mine], r2s.at[d - 1], r2r.at[d - 1], zs[d], gy))
    start(bcast)
    fin[mine] = acc
    sent(near[0] + near[1])
    for w in range(2):
        for group in second[w]:
            sent(group)
    sent(third)
    for o in range(n):

        @pl.when(gz != owner(o))
        def _():
            give(o).wait_send()


    @pl.when(jnp.logical_not(is_high))
    def _():
        sent(to_high + diag_high)

    @pl.when(jnp.logical_not(is_low))
    def _():
        sent(to_low + diag_low)

    whole = orecv.at[pl.ds(0, count)]
    summed = remote(whole, whole, os.at[0], orr.at[0], up, gy)
    summed.wait_recv()
    obj_out[0, 0] = jnp.sum(orecv[...])
    arrived(bcast)
    for b in range(tiles * lanes):
        sens_out[pl.ds(b // lanes * 8, 8), pl.ds(b % lanes * 128, 128)] = fin[b // per, b % per]
    sent(bcast)
    summed.wait_send()


def store(fields, sens, fields_out, sens_out, sem):
    copies = [pltpu.make_async_copy(fields.at[k], fields_out.at[k], sem.at[k]) for k in range(6)]
    copies.append(pltpu.make_async_copy(sens, sens_out, sem.at[6]))
    for copy in copies:
        copy.start()
    for copy in copies:
        copy.wait()


def solution(mesh):
    n, m = mesh.shape["gz"], mesh.shape["gy"]

    def on_device(phase, solute, labels, quat_table, heat_map, cotangent):
        depth, rows, cols = phase.shape
        blocks = rows // 8 * (cols // 128)
        per = -(-blocks // n)
        tall = rows + 16
        vmem = pl.BlockSpec(memory_space=pltpu.VMEM)
        hbm = pl.BlockSpec(memory_space=pltpu.HBM)
        smem = pl.BlockSpec(memory_space=pltpu.SMEM)
        fine = pltpu.SemaphoreType.DMA((4, rows // 8))
        dma = lambda k: pltpu.SemaphoreType.DMA((k,))
        final, sens, obj = pl.pallas_call(
            functools.partial(kernel, n, m, depth, rows, cols, per),
            out_shape=(
                pltpu.VMEM((6, depth, rows, cols), F32),
                pltpu.VMEM((rows, cols), F32),
                jax.ShapeDtypeStruct((1, 1), F32),
            ),
            in_specs=[hbm, hbm, hbm, smem, hbm, hbm],
            out_specs=(vmem, vmem, smem),
            scratch_shapes=[
                pltpu.VMEM((6, depth + 2, tall, cols), F32),
                pltpu.VMEM((depth + 2, tall, cols), jnp.int32),
                pltpu.VMEM((6, depth + 2, tall, cols), F32),
                pltpu.VMEM((2, depth + 2, tall, cols), F32),
                pltpu.VMEM((depth + 2, tall, cols), F32),
                pltpu.VMEM((4, depth, rows, cols), F32),
                pltpu.VMEM((depth + 2, tall, cols), F32),
                pltpu.VMEM((2, rows, cols), F32),
                pltpu.VMEM((2, rows, cols), jnp.int32),
                pltpu.VMEM((2, rows, cols), F32),
                pltpu.VMEM((tall, cols), F32),
                pltpu.VMEM((4, 8, 128), F32),
                pltpu.VMEM((n * per, 8, 128), F32),
                pltpu.VMEM((n, per, 8, 128), F32),
                pltpu.VMEM((8, 128), F32),
                pltpu.VMEM((1, 128), F32),
                pltpu.VMEM((n * m, 128), F32),
                pltpu.VMEM((per, 8, 128), F32),
                pltpu.VMEM((n, per, 8, 128), F32),
                dma(7), dma(12), dma(12), dma(6), dma(6), dma(12), dma(12), fine, fine, dma(2), dma(2),
                dma(n), dma(n), dma(1), dma(1), dma(n - 1), dma(n - 1),
            ],
            compiler_params=pltpu.CompilerParams(
                collective_id=0, has_side_effects=True, vmem_limit_bytes=56 * 1024 * 1024
            ),
        )(phase, solute, labels, quat_table.T, heat_map, cotangent)
        final, sens = pl.pallas_call(
            store,
            out_shape=(
                jax.ShapeDtypeStruct((6, depth, rows, cols), F32),
                jax.ShapeDtypeStruct((rows, cols), F32),
            ),
            in_specs=[vmem, vmem],
            out_specs=(hbm, hbm),
            scratch_shapes=[dma(7)],
            compiler_params=pltpu.CompilerParams(vmem_limit_bytes=4 * 1024 * 1024),
        )(final, sens)
        return final, sens, obj[0, 0]

    return jax.shard_map(
        on_device,
        mesh=mesh,
        in_specs=(
            P("gz", "gy", None),
            P("gz", "gy", None),
            P("gz", "gy", None),
            P(),
            P("gy", None),
            P(None, "gz", "gy", None),
        ),
        out_specs=(P(None, "gz", "gy", None), P("gy", None), P()),
        check_vma=False,
    )
```

```python
import functools

import jax
import jax.numpy as jnp
from jax import lax
from jax.experimental import pallas as pl
from jax.experimental.pallas import tpu as pltpu
from jax.sharding import PartitionSpec as P

MESH = pl.DeviceIdType.MESH
F32 = jnp.float32


def kernel(
    n, m, depth, rows, cols, per,
    phase, solute, labels, quats, heat_in, cot,
    out, sens_out, obj_out,
    E, lab, M, G, GP, CQ, W0, Z2P, Z2L, Z2C, heat, table, sbuf, rbuf, obuf, osend, orecv, red, fin,
    lsem, ysend, yrecv, zsend, zrecv, dsend, drecv, fsend, frecv, csend, crecv, r1s, r1r, os, orr, r2s, r2r,
):
    gz = lax.axis_index("gz")
    gy = lax.axis_index("gy")
    zs = [lax.rem(gz + d, n) for d in range(n)]
    ys = [lax.rem(gy + d, m) for d in range(m)]
    up, down = zs[1], zs[n - 1]
    is_low = gy == 0
    is_high = gy == m - 1
    low = jnp.maximum(gy - 1, 0)
    high = jnp.minimum(gy + 1, m - 1)
    tiles = rows // 8
    lanes = cols // 128
    D = depth
    own = pl.ds(8, rows)
    top = 8 + rows
    others = [(a, b) for a in range(n) for b in range(m) if a or b]

    bar = pltpu.get_barrier_semaphore()
    for a, b in others:
        pl.semaphore_signal(bar, inc=1, device_id=(zs[a], ys[b]), device_id_type=MESH)

    local = []
    dests = ((labels, lab), (phase, E.at[0]), (solute, E.at[5]))
    for k, (src, dst) in enumerate(dests):
        local.append(pltpu.make_async_copy(src, dst.at[pl.ds(1, D), own], lsem.at[k]))
    local.append(pltpu.make_async_copy(cot.at[0], G.at[0, pl.ds(1, D), own], lsem.at[3]))
    local.append(pltpu.make_async_copy(cot.at[5], G.at[1, pl.ds(1, D), own], lsem.at[4]))
    local.append(pltpu.make_async_copy(cot.at[pl.ds(1, 4)], CQ, lsem.at[5]))
    local.append(pltpu.make_async_copy(heat_in, heat.at[own], lsem.at[6]))
    for copy in local:
        copy.start()

    def remote(src, dst, ss, rs, z, y):
        return pltpu.make_async_remote_copy(
            src_ref=src, dst_ref=dst, send_sem=ss, recv_sem=rs, device_id=(z, y), device_id_type=MESH
        )

    odd = lax.rem(gz, 2)
    halo = ((D + 1) * (1 - odd), (D + 1) * odd)
    edge = (1 + (D - 1) * (1 - odd), 1 + (D - 1) * odd)
    into = (halo[1], halo[0])
    mate = (jnp.where(odd == 0, up, down), jnp.where(odd == 0, down, up))
    outer = (edge[0] - 1, edge[1] - 1)
    deeper = (1 + (D - 3) * (1 - odd), 1 + (D - 3) * odd)

    def nearest(w):
        return [
            remote(src.at[outer[w]], dst.at[into[w], own], zsend.at[2 * k + w], zrecv.at[2 * k + w], mate[w], gy)
            for k, (src, dst) in enumerate(dests)
        ]

    near = (nearest(0), nearest(1))
    to_high, to_low = [], []
    faces = [(s, d, 2) for s, d in dests] + [(cot.at[0], G.at[0], 1), (cot.at[5], G.at[1], 1)]
    inner = pl.ds(1, D)
    for k, (src, dst, w) in enumerate(faces):
        to_high.append(
            remote(
                src.at[:, pl.ds(rows - w, w)], dst.at[inner, pl.ds(8 - w, w)], ysend.at[k], yrecv.at[k], gz, high
            )
        )
        to_low.append(
            remote(src.at[:, pl.ds(0, w)], dst.at[inner, pl.ds(top, w)], ysend.at[6 + k], yrecv.at[6 + k], gz, low)
        )
    to_high.append(
        remote(heat_in.at[pl.ds(rows - 1, 1)], heat.at[pl.ds(7, 1)], ysend.at[5], yrecv.at[5], gz, high)
    )
    to_low.append(remote(heat_in.at[pl.ds(0, 1)], heat.at[pl.ds(top, 1)], ysend.at[11], yrecv.at[11], gz, low))
    first, last = pl.ds(0, 1), pl.ds(rows - 1, 1)
    before, after = pl.ds(7, 1), pl.ds(top, 1)
    diag_high, diag_low = [], []
    for k, (src, dst) in enumerate(dests):
        i = 2 * k
        diag_high.append(remote(src.at[D - 1, last], dst.at[0, before], dsend.at[i], drecv.at[i], up, high))
        diag_low.append(remote(src.at[D - 1, first], dst.at[0, after], dsend.at[6 + i], drecv.at[6 + i], up, low))
        i += 1
        diag_high.append(remote(src.at[0, last], dst.at[D + 1, before], dsend.at[i], drecv.at[i], down, high))
        diag_low.append(
            remote(src.at[0, first], dst.at[D + 1, after], dsend.at[6 + i], drecv.at[6 + i], down, low)
        )

    def distant(w):
        found = []
        for t in range(tiles):
            a = pl.ds(t * 8, 8)
            found.append([
                remote(src.at[deeper[w], a], dst.at[w, a], fsend.at[2 * k + w, t], frecv.at[2 * k + w, t], mate[w], gy)
                for k, (src, dst) in enumerate(((labels, Z2L), (phase, Z2P)))
            ])
        return found

    second = (distant(0), distant(1))
    third = [
        remote(solute.at[deeper[w]], Z2C.at[w], csend.at[w], crecv.at[w], mate[w], gy) for w in range(2)
    ]

    def start(copies):
        for copy in copies:
            copy.start()

    def sent(copies):
        for copy in copies:
            copy.wait_send()

    def arrived(copies):
        for copy in copies:
            copy.wait_recv()

    pl.semaphore_wait(bar, n * m - 1)
    @pl.when(jnp.logical_not(is_high))
    def _():
        start(diag_high + to_high)

    @pl.when(jnp.logical_not(is_low))
    def _():
        start(diag_low + to_low)

    start(near[1])

    start(near[0])

    for w in (1, 0):
        for group in second[w]:
            start(group)
    start(third[:1])

    row = lax.broadcasted_iota(jnp.int32, (8, 128), 0)
    lane = lax.broadcasted_iota(jnp.int32, (8, 128), 1)
    zero = jnp.zeros((8, 128), F32)

    for k in range(4):
        entry = zero
        for grain in range(quats.shape[1]):
            entry = jnp.where(lane == grain, quats[k, grain], entry)
        table[k] = entry
    sbuf[...] = jnp.zeros_like(sbuf)
    obuf[...] = jnp.zeros_like(obuf)
    for z in (0, D + 1):
        G[1, z] = jnp.zeros((rows + 16, cols), F32)
        GP[z] = jnp.zeros((rows + 16, cols), F32)

    def ds8(t):
        return pl.ds(pl.multiple_of(t * 8, 8), 8)

    def expand(z, t):
        r = ds8(t)
        for j in range(lanes):
            x = pl.ds(j * 128, 128)
            ids = lab[z, r, x]
            for k in range(4):
                E[1 + k, z, r, x] = jnp.take_along_axis(table[k], ids, axis=1)

    def wipe(z, t):
        r = ds8(t)
        for k in range(6):
            E[k, z, r, :] = jnp.zeros((8, cols), F32)

    def loop(count, body):
        def step(i, carry):
            body(i)
            return carry

        lax.fori_loop(0, count, step, 0)

    def around(ref, lead, z, t, j, toward=None):
        r, x = ds8(t), pl.ds(j * 128, 128)
        c = ref[(*lead, z, r, x)]
        above = ref[(*lead, z, ds8(jnp.maximum(t - 1, 0)), x)]
        below = ref[(*lead, z, ds8(jnp.minimum(t + 1, tiles + 1)), x)]
        left = ref[(*lead, z, r, pl.ds((j - 1) * 128, 128))] if j else zero
        right = ref[(*lead, z, r, pl.ds((j + 1) * 128, 128))] if j < lanes - 1 else zero
        ysum = pltpu.roll(jnp.where(row == 0, below, c), 7, 0) + pltpu.roll(jnp.where(row == 7, above, c), 1, 0)
        xsum = pltpu.roll(jnp.where(lane == 0, right, c), 127, 1) + pltpu.roll(jnp.where(lane == 127, left, c), 1, 1)
        if toward is None:
            zsum = ref[(*lead, z + 1, r, x)] + ref[(*lead, z - 1, r, x)]
        else:
            zsum = ref[(*lead, z + toward, r, x)]
        return c, zsum + ysum + xsum - 6.0 * c

    def keeping(t):
        drop = ((t == 0) & is_low) | ((t == tiles + 1) & is_high)
        return jnp.where(drop, 0.0, 1.0)

    def mid(z, t, inside, toward=None):
        r = ds8(t)
        keep = keeping(t)
        for j in range(lanes):
            x = pl.ds(j * 128, 128)
            p, lp = around(E, (0,), z, t, j, toward)
            c, lc = around(E, (5,), z, t, j, toward)
            misfit = zero
            rate = 0.08 * ((1.0 - p) * (1.0 - p) + 0.1)
            for k in range(4):
                q, lq = around(E, (1 + k,), z, t, j, toward)
                misfit = misfit + q * lq
                M[1 + k, z, r, x] = keep * (q + rate * lq)
            th = jnp.tanh(heat[r, x] - 0.5 * c)
            pq = p * (1.0 - p)
            dp = 0.08 * (lp + 4.0 * pq * (p - 0.5 + 0.6 * th) + 0.2 * p * misfit)
            cn = keep * (c + 0.064 * lc + 0.5 * dp * c)
            M[0, z, r, x] = keep * (p + dp)
            M[5, z, r, x] = cn
            W0[z, r, x] = 0.192 * pq * (1.0 - th * th)
            if inside:
                GP[z, r, x] = G[0, z, r, x] + 0.5 * cn * G[1, z, r, x]

    def bump(z, t, other):
        r = ds8(t)
        keep = keeping(t)
        for j in range(lanes):
            x = pl.ds(j * 128, 128)
            p = E[0, z, r, x]
            rate = keep * (0.08 * ((1.0 - p) * (1.0 - p) + 0.1))
            misfit = zero
            for k in range(4):
                q = E[1 + k, other, r, x]
                misfit = misfit + E[1 + k, z, r, x] * q
                M[1 + k, z, r, x] += rate * q
            dp = 0.08 * (E[0, other, r, x] + 0.2 * p * misfit)
            dc = keep * (0.064 * E[5, other, r, x] + 0.5 * dp * E[5, z, r, x])
            M[0, z, r, x] += keep * dp
            M[5, z, r, x] += dc
            GP[z, r, x] += 0.5 * dc * G[1, z, r, x]

    def bump_far(z, t, side):
        r, ro = ds8(t), ds8(t - 1)
        for j in range(lanes):
            x = pl.ds(j * 128, 128)
            p = E[0, z, r, x]
            rate = 0.08 * ((1.0 - p) * (1.0 - p) + 0.1)
            misfit = zero
            ids = Z2L[side, ro, x]
            for k in range(4):
                q = jnp.take_along_axis(table[k], ids, axis=1)
                misfit = misfit + E[1 + k, z, r, x] * q
                M[1 + k, z, r, x] += rate * q
            dp = 0.08 * (Z2P[side, ro, x] + 0.2 * p * misfit)
            M[0, z, r, x] += dp
            M[5, z, r, x] += 0.5 * dp * E[5, z, r, x]

    def final(z, t, edge):
        r = ds8(t)
        ro = ds8(t - 1)
        objective = zero
        for j in range(lanes):
            x = pl.ds(j * 128, 128)
            p, lp = around(M, (0,), z, t, j)
            c, lc = around(M, (5,), z, t, j)
            gc, lgc = around(G, (1,), z, t, j)
            gp, lgp = around(GP, (), z, t, j)
            g0 = G[0, z, r, x]
            rate = 0.08 * ((1.0 - p) * (1.0 - p) + 0.1)
            misfit, qterm = zero, zero
            for k in range(4):
                q, lq = around(M, (1 + k,), z, t, j)
                g = CQ[k, z - 1, ro, x]
                qn = q + rate * lq
                out[1 + k, z - 1, ro, x] = qn
                misfit = misfit + q * lq
                qterm = qterm + g * lq
                objective = objective + g * qn
            th = jnp.tanh(heat[r, x] - 0.5 * c)
            pq = p * (1.0 - p)
            drive = p - 0.5 + 0.6 * th
            dp = 0.08 * (lp + 4.0 * pq * drive + 0.2 * p * misfit)
            pn = p + dp
            cn = c + 0.064 * lc + 0.5 * dp * c
            out[0, z - 1, ro, x] = pn
            out[5, z - 1, ro, x] = cn
            objective = objective + g0 * pn + gc * cn
            w = 0.192 * pq * (1.0 - th * th)
            gw = gp * w
            lam_p = (
                gp * (1.0 + 0.08 * (4.0 * (1.0 - 2.0 * p) * drive + 4.0 * pq + 0.2 * misfit))
                + 0.08 * lgp
                - 0.5 * c * gc
                - 0.16 * (1.0 - p) * qterm
            )
            lam_c = gc * (1.0 + 0.5 * dp) + 0.064 * lgc - 0.5 * gw
            s = gw + (lam_p + 0.5 * E[5, z, r, x] * lam_c) * W0[z, r, x]
            if edge is not None:
                s = s + W0[edge, r, x] * (0.08 * gp + 0.032 * E[5, edge, r, x] * gc)
            sbuf[(t - 1) * lanes + j] += s
        obuf[...] += objective

    arrived_local = local[:3]
    for copy in arrived_local:
        copy.wait()
    loop(D * tiles, lambda i: expand(1 + i // tiles, 1 + i % tiles))

    @pl.when(jnp.logical_not(is_low))
    def _():
        arrived(to_high)
        loop(D, lambda i: expand(1 + i, 0))

    @pl.when(is_low)
    def _():
        loop(D + 2, lambda i: wipe(i, 0))
        heat[pl.ds(0, 8), :] = jnp.zeros((8, cols), F32)
        for k in range(2):
            for z in range(D):
                G[k, 1 + z, pl.ds(0, 8), :] = jnp.zeros((8, cols), F32)

    @pl.when(jnp.logical_not(is_high))
    def _():
        arrived(to_low)
        loop(D, lambda i: expand(1 + i, tiles + 1))

    @pl.when(is_high)
    def _():
        loop(D + 2, lambda i: wipe(i, tiles + 1))
        heat[pl.ds(top, 8), :] = jnp.zeros((8, cols), F32)
        for k in range(2):
            for z in range(D):
                G[k, 1 + z, pl.ds(top, 8), :] = jnp.zeros((8, cols), F32)

    for copy in local[3:]:
        copy.wait()
    tall = tiles + 2
    loop((D - 2) * tall, lambda i: mid(2 + i // tall, i % tall, True))
    loop(2 * tall, lambda i: mid(1 + (D - 1) * (i // tall), i % tall, True, 1 - 2 * (i // tall)))

    @pl.when(jnp.logical_not(is_low))
    def _():
        arrived(diag_high)
        loop(2, lambda i: expand((D + 1) * i, 0))

    @pl.when(jnp.logical_not(is_high))
    def _():
        arrived(diag_low)
        loop(2, lambda i: expand((D + 1) * i, tiles + 1))

    def join(w):
        arrived(near[w])
        loop(tiles, lambda i: expand(halo[w], 1 + i))
        loop(tall, lambda i: bump(edge[w], i, halo[w]))
        loop(tiles, lambda i: mid(halo[w], 1 + i, False, edge[w] - halo[w]))

    step = halo[0] - edge[0]
    join(1)
    for t in range(tiles):
        arrived(second[1][t])
    loop(tiles, lambda i: bump_far(halo[1], 1 + i, 1))
    loop(tiles, lambda i: final(edge[1], 1 + i, halo[1]))
    loop((D - 3) * tiles, lambda i: final(edge[1] + step * (1 + i // tiles), 1 + i % tiles, None))
    join(0)
    loop(tiles, lambda i: final(edge[0] - step, 1 + i, None))

    mine = lax.rem(gz + n - n // 2 - 1, n)

    def owner(o):
        return (o + n // 2 + 1) % n

    def give(o):
        return remote(sbuf.at[pl.ds(o * per, per)], rbuf.at[gz], r1s.at[o], r1r.at[gz], owner(o), gy)

    def take(o):
        return remote(sbuf.at[pl.ds(o * per, per)], rbuf.at[o], r1s.at[o], r1r.at[o], o, gy)

    def partners(action):
        for o in range(n):

            @pl.when(gz != o)
            def _():
                action(o)

    given = 0
    for t in range(tiles):
        arrived(second[0][t])
        if t == tiles - 2:
            start(third[1:])
        bump_far(halo[0], t + 1, 0)
        final(edge[0], t + 1, halo[0])
        ready = n if t == tiles - 1 else (t + 1) * lanes // per
        for o in range(given, ready):

            @pl.when(gz != owner(o))
            def _():
                give(o).start()

        given = ready

    for side in (1, 0):
        arrived([third[side]])

        def correct(t, side=side):
            r, ro = ds8(t + 1), ds8(t)
            objective = zero
            for j in range(lanes):
                x = pl.ds(j * 128, 128)
                dc = 0.064 * 0.064 * Z2C[side, ro, x]
                out[5, outer[side], ro, x] += dc
                objective = objective + dc * G[1, edge[side], r, x]
            obuf[...] += objective

        loop(tiles, correct)

    total = jnp.sum(obuf[...], axis=0, keepdims=True)
    osend[...] = total
    count = n * m - 1
    orecv[pl.ds(count, 1)] = total
    for i, (a, b) in enumerate(others):
        remote(osend, orecv.at[pl.ds(i, 1)], os.at[0], orr.at[0], zs[a], ys[b]).start()

    rbuf[gz] = sbuf[pl.ds(mine * per, per)]
    partners(lambda o: take(o).wait_recv())
    acc = rbuf[0]
    for d in range(1, n):
        acc = acc + rbuf[d]
    red[...] = acc
    bcast = []
    for d in range(1, n):
        bcast.append(remote(red, fin.at[mine], r2s.at[d - 1], r2r.at[d - 1], zs[d], gy))
    start(bcast)
    fin[mine] = acc
    sent(near[0] + near[1])
    for w in range(2):
        for group in second[w]:
            sent(group)
    sent(third)
    for o in range(n):

        @pl.when(gz != owner(o))
        def _():
            give(o).wait_send()


    @pl.when(jnp.logical_not(is_high))
    def _():
        sent(to_high + diag_high)

    @pl.when(jnp.logical_not(is_low))
    def _():
        sent(to_low + diag_low)

    whole = orecv.at[pl.ds(0, count)]
    summed = remote(whole, whole, os.at[0], orr.at[0], up, gy)
    summed.wait_recv()
    obj_out[0, 0] = jnp.sum(orecv[...])
    arrived(bcast)
    for b in range(tiles * lanes):
        sens_out[pl.ds(b // lanes * 8, 8), pl.ds(b % lanes * 128, 128)] = fin[b // per, b % per]
    sent(bcast)
    summed.wait_send()


def store(fields, sens, fields_out, sens_out, sem):
    copies = [pltpu.make_async_copy(fields.at[k], fields_out.at[k], sem.at[k]) for k in range(6)]
    copies.append(pltpu.make_async_copy(sens, sens_out, sem.at[6]))
    for copy in copies:
        copy.start()
    for copy in copies:
        copy.wait()


def solution(mesh):
    n, m = mesh.shape["gz"], mesh.shape["gy"]

    def on_device(phase, solute, labels, quat_table, heat_map, cotangent):
        depth, rows, cols = phase.shape
        blocks = rows // 8 * (cols // 128)
        per = -(-blocks // n)
        tall = rows + 16
        vmem = pl.BlockSpec(memory_space=pltpu.VMEM)
        hbm = pl.BlockSpec(memory_space=pltpu.HBM)
        smem = pl.BlockSpec(memory_space=pltpu.SMEM)
        fine = pltpu.SemaphoreType.DMA((4, rows // 8))
        dma = lambda k: pltpu.SemaphoreType.DMA((k,))
        final, sens, obj = pl.pallas_call(
            functools.partial(kernel, n, m, depth, rows, cols, per),
            out_shape=(
                pltpu.VMEM((6, depth, rows, cols), F32),
                pltpu.VMEM((rows, cols), F32),
                jax.ShapeDtypeStruct((1, 1), F32),
            ),
            in_specs=[hbm, hbm, hbm, smem, hbm, hbm],
            out_specs=(vmem, vmem, smem),
            scratch_shapes=[
                pltpu.VMEM((6, depth + 2, tall, cols), F32),
                pltpu.VMEM((depth + 2, tall, cols), jnp.int32),
                pltpu.VMEM((6, depth + 2, tall, cols), F32),
                pltpu.VMEM((2, depth + 2, tall, cols), F32),
                pltpu.VMEM((depth + 2, tall, cols), F32),
                pltpu.VMEM((4, depth, rows, cols), F32),
                pltpu.VMEM((depth + 2, tall, cols), F32),
                pltpu.VMEM((2, rows, cols), F32),
                pltpu.VMEM((2, rows, cols), jnp.int32),
                pltpu.VMEM((2, rows, cols), F32),
                pltpu.VMEM((tall, cols), F32),
                pltpu.VMEM((4, 8, 128), F32),
                pltpu.VMEM((n * per, 8, 128), F32),
                pltpu.VMEM((n, per, 8, 128), F32),
                pltpu.VMEM((8, 128), F32),
                pltpu.VMEM((1, 128), F32),
                pltpu.VMEM((n * m, 128), F32),
                pltpu.VMEM((per, 8, 128), F32),
                pltpu.VMEM((n, per, 8, 128), F32),
                dma(7), dma(12), dma(12), dma(6), dma(6), dma(12), dma(12), fine, fine, dma(2), dma(2),
                dma(n), dma(n), dma(1), dma(1), dma(n - 1), dma(n - 1),
            ],
            compiler_params=pltpu.CompilerParams(
                collective_id=0, has_side_effects=True, vmem_limit_bytes=56 * 1024 * 1024
            ),
        )(phase, solute, labels, quat_table.T, heat_map, cotangent)
        final, sens = pl.pallas_call(
            store,
            out_shape=(
                jax.ShapeDtypeStruct((6, depth, rows, cols), F32),
                jax.ShapeDtypeStruct((rows, cols), F32),
            ),
            in_specs=[vmem, vmem],
            out_specs=(hbm, hbm),
            scratch_shapes=[dma(7)],
            compiler_params=pltpu.CompilerParams(vmem_limit_bytes=4 * 1024 * 1024),
        )(final, sens)
        return final, sens, obj[0, 0]

    return jax.shard_map(
        on_device,
        mesh=mesh,
        in_specs=(
            P("gz", "gy", None),
            P("gz", "gy", None),
            P("gz", "gy", None),
            P(),
            P("gy", None),
            P(None, "gz", "gy", None),
        ),
        out_specs=(P(None, "gz", "gy", None), P("gy", None), P()),
        check_vma=False,
    )
```

```python
import functools

import jax
import jax.numpy as jnp
from jax import lax
from jax.experimental import pallas as pl
from jax.experimental.pallas import tpu as pltpu
from jax.sharding import PartitionSpec as P

MESH = pl.DeviceIdType.MESH
F32 = jnp.float32


def kernel(
    n, m, depth, rows, cols, per,
    phase, solute, labels, quats, heat_in, cot,
    out, sens_out, obj_out,
    E, lab, M, G, GP, CQ, W0, Z2P, Z2L, Z2C, heat, table, sbuf, rbuf, obuf, osend, orecv, red, fin,
    lsem, ysend, yrecv, zsend, zrecv, dsend, drecv, fsend, frecv, csend, crecv, r1s, r1r, os, orr, r2s, r2r,
):
    gz = lax.axis_index("gz")
    gy = lax.axis_index("gy")
    zs = [lax.rem(gz + d, n) for d in range(n)]
    ys = [lax.rem(gy + d, m) for d in range(m)]
    up, down = zs[1], zs[n - 1]
    is_low = gy == 0
    is_high = gy == m - 1
    low = jnp.maximum(gy - 1, 0)
    high = jnp.minimum(gy + 1, m - 1)
    tiles = rows // 8
    lanes = cols // 128
    D = depth
    own = pl.ds(8, rows)
    top = 8 + rows
    others = [(a, b) for a in range(n) for b in range(m) if a or b]

    bar = pltpu.get_barrier_semaphore()
    for a, b in others:
        pl.semaphore_signal(bar, inc=1, device_id=(zs[a], ys[b]), device_id_type=MESH)

    local = []
    dests = ((labels, lab), (phase, E.at[0]), (solute, E.at[5]))
    for k, (src, dst) in enumerate(dests):
        local.append(pltpu.make_async_copy(src, dst.at[pl.ds(1, D), own], lsem.at[k]))
    local.append(pltpu.make_async_copy(cot.at[0], G.at[0, pl.ds(1, D), own], lsem.at[3]))
    local.append(pltpu.make_async_copy(cot.at[5], G.at[1, pl.ds(1, D), own], lsem.at[4]))
    local.append(pltpu.make_async_copy(cot.at[pl.ds(1, 4)], CQ, lsem.at[5]))
    local.append(pltpu.make_async_copy(heat_in, heat.at[own], lsem.at[6]))
    for copy in local:
        copy.start()

    def remote(src, dst, ss, rs, z, y):
        return pltpu.make_async_remote_copy(
            src_ref=src, dst_ref=dst, send_sem=ss, recv_sem=rs, device_id=(z, y), device_id_type=MESH
        )

    odd = lax.rem(gz, 2)
    halo = ((D + 1) * (1 - odd), (D + 1) * odd)
    edge = (1 + (D - 1) * (1 - odd), 1 + (D - 1) * odd)
    into = (halo[1], halo[0])
    mate = (jnp.where(odd == 0, up, down), jnp.where(odd == 0, down, up))
    outer = (edge[0] - 1, edge[1] - 1)
    deeper = (1 + (D - 3) * (1 - odd), 1 + (D - 3) * odd)

    def nearest(w):
        return [
            remote(src.at[outer[w]], dst.at[into[w], own], zsend.at[2 * k + w], zrecv.at[2 * k + w], mate[w], gy)
            for k, (src, dst) in enumerate(dests)
        ]

    near = (nearest(0), nearest(1))
    to_high, to_low = [], []
    faces = [(s, d, 2) for s, d in dests] + [(cot.at[0], G.at[0], 1), (cot.at[5], G.at[1], 1)]
    inner = pl.ds(1, D)
    for k, (src, dst, w) in enumerate(faces):
        to_high.append(
            remote(
                src.at[:, pl.ds(rows - w, w)], dst.at[inner, pl.ds(8 - w, w)], ysend.at[k], yrecv.at[k], gz, high
            )
        )
        to_low.append(
            remote(src.at[:, pl.ds(0, w)], dst.at[inner, pl.ds(top, w)], ysend.at[6 + k], yrecv.at[6 + k], gz, low)
        )
    to_high.append(
        remote(heat_in.at[pl.ds(rows - 1, 1)], heat.at[pl.ds(7, 1)], ysend.at[5], yrecv.at[5], gz, high)
    )
    to_low.append(remote(heat_in.at[pl.ds(0, 1)], heat.at[pl.ds(top, 1)], ysend.at[11], yrecv.at[11], gz, low))
    first, last = pl.ds(0, 1), pl.ds(rows - 1, 1)
    before, after = pl.ds(7, 1), pl.ds(top, 1)
    diag_high, diag_low = [], []
    for k, (src, dst) in enumerate(dests):
        i = 2 * k
        diag_high.append(remote(src.at[D - 1, last], dst.at[0, before], dsend.at[i], drecv.at[i], up, high))
        diag_low.append(remote(src.at[D - 1, first], dst.at[0, after], dsend.at[6 + i], drecv.at[6 + i], up, low))
        i += 1
        diag_high.append(remote(src.at[0, last], dst.at[D + 1, before], dsend.at[i], drecv.at[i], down, high))
        diag_low.append(
            remote(src.at[0, first], dst.at[D + 1, after], dsend.at[6 + i], drecv.at[6 + i], down, low)
        )

    def distant(w):
        found = []
        for t in range(tiles):
            a = pl.ds(t * 8, 8)
            found.append([
                remote(src.at[deeper[w], a], dst.at[w, a], fsend.at[2 * k + w, t], frecv.at[2 * k + w, t], mate[w], gy)
                for k, (src, dst) in enumerate(((labels, Z2L), (phase, Z2P)))
            ])
        return found

    second = (distant(0), distant(1))
    third = [
        remote(solute.at[deeper[w]], Z2C.at[w], csend.at[w], crecv.at[w], mate[w], gy) for w in range(2)
    ]

    def start(copies):
        for copy in copies:
            copy.start()

    def sent(copies):
        for copy in copies:
            copy.wait_send()

    def arrived(copies):
        for copy in copies:
            copy.wait_recv()

    pl.semaphore_wait(bar, n * m - 1)
    @pl.when(jnp.logical_not(is_high))
    def _():
        start(diag_high)

    @pl.when(jnp.logical_not(is_low))
    def _():
        start(diag_low)

    start(near[1] + near[0])

    @pl.when(jnp.logical_not(is_high))
    def _():
        start(to_high)

    @pl.when(jnp.logical_not(is_low))
    def _():
        start(to_low)

    for w in (1, 0):
        for group in second[w]:
            start(group)

    row = lax.broadcasted_iota(jnp.int32, (8, 128), 0)
    lane = lax.broadcasted_iota(jnp.int32, (8, 128), 1)
    zero = jnp.zeros((8, 128), F32)

    for k in range(4):
        entry = zero
        for grain in range(quats.shape[1]):
            entry = jnp.where(lane == grain, quats[k, grain], entry)
        table[k] = entry
    sbuf[...] = jnp.zeros_like(sbuf)
    obuf[...] = jnp.zeros_like(obuf)
    for z in (0, D + 1):
        G[1, z] = jnp.zeros((rows + 16, cols), F32)
        GP[z] = jnp.zeros((rows + 16, cols), F32)

    def ds8(t):
        return pl.ds(pl.multiple_of(t * 8, 8), 8)

    def expand(z, t):
        r = ds8(t)
        for j in range(lanes):
            x = pl.ds(j * 128, 128)
            ids = lab[z, r, x]
            for k in range(4):
                E[1 + k, z, r, x] = jnp.take_along_axis(table[k], ids, axis=1)

    def wipe(z, t):
        r = ds8(t)
        for k in range(6):
            E[k, z, r, :] = jnp.zeros((8, cols), F32)

    def loop(count, body):
        def step(i, carry):
            body(i)
            return carry

        lax.fori_loop(0, count, step, 0)

    def around(ref, lead, z, t, j, toward=None):
        r, x = ds8(t), pl.ds(j * 128, 128)
        c = ref[(*lead, z, r, x)]
        above = ref[(*lead, z, ds8(jnp.maximum(t - 1, 0)), x)]
        below = ref[(*lead, z, ds8(jnp.minimum(t + 1, tiles + 1)), x)]
        left = ref[(*lead, z, r, pl.ds((j - 1) * 128, 128))] if j else zero
        right = ref[(*lead, z, r, pl.ds((j + 1) * 128, 128))] if j < lanes - 1 else zero
        ysum = pltpu.roll(jnp.where(row == 0, below, c), 7, 0) + pltpu.roll(jnp.where(row == 7, above, c), 1, 0)
        xsum = pltpu.roll(jnp.where(lane == 0, right, c), 127, 1) + pltpu.roll(jnp.where(lane == 127, left, c), 1, 1)
        if toward is None:
            zsum = ref[(*lead, z + 1, r, x)] + ref[(*lead, z - 1, r, x)]
        else:
            zsum = ref[(*lead, z + toward, r, x)]
        return c, zsum + ysum + xsum - 6.0 * c

    def keeping(t):
        drop = ((t == 0) & is_low) | ((t == tiles + 1) & is_high)
        return jnp.where(drop, 0.0, 1.0)

    def mid(z, t, inside, toward=None):
        r = ds8(t)
        keep = keeping(t)
        for j in range(lanes):
            x = pl.ds(j * 128, 128)
            p, lp = around(E, (0,), z, t, j, toward)
            c, lc = around(E, (5,), z, t, j, toward)
            misfit = zero
            rate = 0.08 * ((1.0 - p) * (1.0 - p) + 0.1)
            for k in range(4):
                q, lq = around(E, (1 + k,), z, t, j, toward)
                misfit = misfit + q * lq
                M[1 + k, z, r, x] = keep * (q + rate * lq)
            th = jnp.tanh(heat[r, x] - 0.5 * c)
            pq = p * (1.0 - p)
            dp = 0.08 * (lp + 4.0 * pq * (p - 0.5 + 0.6 * th) + 0.2 * p * misfit)
            cn = keep * (c + 0.064 * lc + 0.5 * dp * c)
            M[0, z, r, x] = keep * (p + dp)
            M[5, z, r, x] = cn
            W0[z, r, x] = 0.192 * pq * (1.0 - th * th)
            if inside:
                GP[z, r, x] = G[0, z, r, x] + 0.5 * cn * G[1, z, r, x]

    def bump(z, t, other):
        r = ds8(t)
        keep = keeping(t)
        for j in range(lanes):
            x = pl.ds(j * 128, 128)
            p = E[0, z, r, x]
            rate = keep * (0.08 * ((1.0 - p) * (1.0 - p) + 0.1))
            misfit = zero
            for k in range(4):
                q = E[1 + k, other, r, x]
                misfit = misfit + E[1 + k, z, r, x] * q
                M[1 + k, z, r, x] += rate * q
            dp = 0.08 * (E[0, other, r, x] + 0.2 * p * misfit)
            dc = keep * (0.064 * E[5, other, r, x] + 0.5 * dp * E[5, z, r, x])
            M[0, z, r, x] += keep * dp
            M[5, z, r, x] += dc
            GP[z, r, x] += 0.5 * dc * G[1, z, r, x]

    def bump_far(z, t, side):
        r, ro = ds8(t), ds8(t - 1)
        for j in range(lanes):
            x = pl.ds(j * 128, 128)
            p = E[0, z, r, x]
            rate = 0.08 * ((1.0 - p) * (1.0 - p) + 0.1)
            misfit = zero
            ids = Z2L[side, ro, x]
            for k in range(4):
                q = jnp.take_along_axis(table[k], ids, axis=1)
                misfit = misfit + E[1 + k, z, r, x] * q
                M[1 + k, z, r, x] += rate * q
            dp = 0.08 * (Z2P[side, ro, x] + 0.2 * p * misfit)
            M[0, z, r, x] += dp
            M[5, z, r, x] += 0.5 * dp * E[5, z, r, x]

    def final(z, t, edge):
        r = ds8(t)
        ro = ds8(t - 1)
        objective = zero
        for j in range(lanes):
            x = pl.ds(j * 128, 128)
            p, lp = around(M, (0,), z, t, j)
            c, lc = around(M, (5,), z, t, j)
            gc, lgc = around(G, (1,), z, t, j)
            gp, lgp = around(GP, (), z, t, j)
            g0 = G[0, z, r, x]
            rate = 0.08 * ((1.0 - p) * (1.0 - p) + 0.1)
            misfit, qterm = zero, zero
            for k in range(4):
                q, lq = around(M, (1 + k,), z, t, j)
                g = CQ[k, z - 1, ro, x]
                qn = q + rate * lq
                out[1 + k, z - 1, ro, x] = qn
                misfit = misfit + q * lq
                qterm = qterm + g * lq
                objective = objective + g * qn
            th = jnp.tanh(heat[r, x] - 0.5 * c)
            pq = p * (1.0 - p)
            drive = p - 0.5 + 0.6 * th
            dp = 0.08 * (lp + 4.0 * pq * drive + 0.2 * p * misfit)
            pn = p + dp
            cn = c + 0.064 * lc + 0.5 * dp * c
            out[0, z - 1, ro, x] = pn
            out[5, z - 1, ro, x] = cn
            objective = objective + g0 * pn + gc * cn
            w = 0.192 * pq * (1.0 - th * th)
            gw = gp * w
            lam_p = (
                gp * (1.0 + 0.08 * (4.0 * (1.0 - 2.0 * p) * drive + 4.0 * pq + 0.2 * misfit))
                + 0.08 * lgp
                - 0.5 * c * gc
                - 0.16 * (1.0 - p) * qterm
            )
            lam_c = gc * (1.0 + 0.5 * dp) + 0.064 * lgc - 0.5 * gw
            s = gw + (lam_p + 0.5 * E[5, z, r, x] * lam_c) * W0[z, r, x]
            if edge is not None:
                s = s + W0[edge, r, x] * (0.08 * gp + 0.032 * E[5, edge, r, x] * gc)
            sbuf[(t - 1) * lanes + j] += s
        obuf[...] += objective

    arrived_local = local[:3]
    for copy in arrived_local:
        copy.wait()
    loop(D * tiles, lambda i: expand(1 + i // tiles, 1 + i % tiles))

    @pl.when(jnp.logical_not(is_low))
    def _():
        arrived(to_high)
        loop(D, lambda i: expand(1 + i, 0))

    @pl.when(is_low)
    def _():
        loop(D + 2, lambda i: wipe(i, 0))
        heat[pl.ds(0, 8), :] = jnp.zeros((8, cols), F32)
        for k in range(2):
            for z in range(D):
                G[k, 1 + z, pl.ds(0, 8), :] = jnp.zeros((8, cols), F32)

    @pl.when(jnp.logical_not(is_high))
    def _():
        arrived(to_low)
        loop(D, lambda i: expand(1 + i, tiles + 1))

    @pl.when(is_high)
    def _():
        loop(D + 2, lambda i: wipe(i, tiles + 1))
        heat[pl.ds(top, 8), :] = jnp.zeros((8, cols), F32)
        for k in range(2):
            for z in range(D):
                G[k, 1 + z, pl.ds(top, 8), :] = jnp.zeros((8, cols), F32)

    for copy in local[3:]:
        copy.wait()
    tall = tiles + 2
    loop((D - 2) * tall, lambda i: mid(2 + i // tall, i % tall, True))
    loop(2 * tall, lambda i: mid(1 + (D - 1) * (i // tall), i % tall, True, 1 - 2 * (i // tall)))

    @pl.when(jnp.logical_not(is_low))
    def _():
        arrived(diag_high)
        loop(2, lambda i: expand((D + 1) * i, 0))

    @pl.when(jnp.logical_not(is_high))
    def _():
        arrived(diag_low)
        loop(2, lambda i: expand((D + 1) * i, tiles + 1))

    def join(w):
        arrived(near[w])
        loop(tiles, lambda i: expand(halo[w], 1 + i))
        loop(tall, lambda i: bump(edge[w], i, halo[w]))
        loop(tiles, lambda i: mid(halo[w], 1 + i, False, edge[w] - halo[w]))

    step = halo[0] - edge[0]
    join(1)
    for t in range(tiles):
        arrived(second[1][t])
    loop(tiles, lambda i: bump_far(halo[1], 1 + i, 1))
    loop(tiles, lambda i: final(edge[1], 1 + i, halo[1]))
    loop((D - 3) * tiles, lambda i: final(edge[1] + step * (1 + i // tiles), 1 + i % tiles, None))
    join(0)
    loop(tiles, lambda i: final(edge[0] - step, 1 + i, None))

    mine = lax.rem(gz + n - n // 2 - 1, n)

    def owner(o):
        return (o + n // 2 + 1) % n

    def give(o):
        return remote(sbuf.at[pl.ds(o * per, per)], rbuf.at[gz], r1s.at[o], r1r.at[gz], owner(o), gy)

    def take(o):
        return remote(sbuf.at[pl.ds(o * per, per)], rbuf.at[o], r1s.at[o], r1r.at[o], o, gy)

    def partners(action):
        for o in range(n):

            @pl.when(gz != o)
            def _():
                action(o)

    given = 0
    for t in range(tiles):
        arrived(second[0][t])
        if t == tiles - 2:
            start(third)
        bump_far(halo[0], t + 1, 0)
        final(edge[0], t + 1, halo[0])
        ready = n if t == tiles - 1 else (t + 1) * lanes // per
        for o in range(given, ready):

            @pl.when(gz != owner(o))
            def _():
                give(o).start()

        given = ready

    for side in (1, 0):
        arrived([third[side]])

        def correct(t, side=side):
            r, ro = ds8(t + 1), ds8(t)
            objective = zero
            for j in range(lanes):
                x = pl.ds(j * 128, 128)
                dc = 0.064 * 0.064 * Z2C[side, ro, x]
                out[5, outer[side], ro, x] += dc
                objective = objective + dc * G[1, edge[side], r, x]
            obuf[...] += objective

        loop(tiles, correct)

    total = jnp.sum(obuf[...], axis=0, keepdims=True)
    osend[...] = total
    count = n * m - 1
    orecv[pl.ds(count, 1)] = total
    for i, (a, b) in enumerate(others):
        remote(osend, orecv.at[pl.ds(i, 1)], os.at[0], orr.at[0], zs[a], ys[b]).start()

    rbuf[gz] = sbuf[pl.ds(mine * per, per)]
    partners(lambda o: take(o).wait_recv())
    acc = rbuf[0]
    for d in range(1, n):
        acc = acc + rbuf[d]
    red[...] = acc
    bcast = []
    for d in range(1, n):
        bcast.append(remote(red, fin.at[mine], r2s.at[d - 1], r2r.at[d - 1], zs[d], gy))
    start(bcast)
    fin[mine] = acc
    sent(near[0] + near[1])
    for w in range(2):
        for group in second[w]:
            sent(group)
    sent(third)
    for o in range(n):

        @pl.when(gz != owner(o))
        def _():
            give(o).wait_send()


    @pl.when(jnp.logical_not(is_high))
    def _():
        sent(to_high + diag_high)

    @pl.when(jnp.logical_not(is_low))
    def _():
        sent(to_low + diag_low)

    whole = orecv.at[pl.ds(0, count)]
    summed = remote(whole, whole, os.at[0], orr.at[0], up, gy)
    summed.wait_recv()
    obj_out[0, 0] = jnp.sum(orecv[...])
    arrived(bcast)
    for b in range(tiles * lanes):
        sens_out[pl.ds(b // lanes * 8, 8), pl.ds(b % lanes * 128, 128)] = fin[b // per, b % per]
    sent(bcast)
    summed.wait_send()


def store(fields, sens, fields_out, sens_out, sem):
    copies = [pltpu.make_async_copy(fields.at[k], fields_out.at[k], sem.at[k]) for k in range(6)]
    copies.append(pltpu.make_async_copy(sens, sens_out, sem.at[6]))
    for copy in copies:
        copy.start()
    for copy in copies:
        copy.wait()


def solution(mesh):
    n, m = mesh.shape["gz"], mesh.shape["gy"]

    def on_device(phase, solute, labels, quat_table, heat_map, cotangent):
        depth, rows, cols = phase.shape
        blocks = rows // 8 * (cols // 128)
        per = -(-blocks // n)
        tall = rows + 16
        vmem = pl.BlockSpec(memory_space=pltpu.VMEM)
        hbm = pl.BlockSpec(memory_space=pltpu.HBM)
        smem = pl.BlockSpec(memory_space=pltpu.SMEM)
        fine = pltpu.SemaphoreType.DMA((4, rows // 8))
        dma = lambda k: pltpu.SemaphoreType.DMA((k,))
        final, sens, obj = pl.pallas_call(
            functools.partial(kernel, n, m, depth, rows, cols, per),
            out_shape=(
                pltpu.VMEM((6, depth, rows, cols), F32),
                pltpu.VMEM((rows, cols), F32),
                jax.ShapeDtypeStruct((1, 1), F32),
            ),
            in_specs=[hbm, hbm, hbm, smem, hbm, hbm],
            out_specs=(vmem, vmem, smem),
            scratch_shapes=[
                pltpu.VMEM((6, depth + 2, tall, cols), F32),
                pltpu.VMEM((depth + 2, tall, cols), jnp.int32),
                pltpu.VMEM((6, depth + 2, tall, cols), F32),
                pltpu.VMEM((2, depth + 2, tall, cols), F32),
                pltpu.VMEM((depth + 2, tall, cols), F32),
                pltpu.VMEM((4, depth, rows, cols), F32),
                pltpu.VMEM((depth + 2, tall, cols), F32),
                pltpu.VMEM((2, rows, cols), F32),
                pltpu.VMEM((2, rows, cols), jnp.int32),
                pltpu.VMEM((2, rows, cols), F32),
                pltpu.VMEM((tall, cols), F32),
                pltpu.VMEM((4, 8, 128), F32),
                pltpu.VMEM((n * per, 8, 128), F32),
                pltpu.VMEM((n, per, 8, 128), F32),
                pltpu.VMEM((8, 128), F32),
                pltpu.VMEM((1, 128), F32),
                pltpu.VMEM((n * m, 128), F32),
                pltpu.VMEM((per, 8, 128), F32),
                pltpu.VMEM((n, per, 8, 128), F32),
                dma(7), dma(12), dma(12), dma(6), dma(6), dma(12), dma(12), fine, fine, dma(2), dma(2),
                dma(n), dma(n), dma(1), dma(1), dma(n - 1), dma(n - 1),
            ],
            compiler_params=pltpu.CompilerParams(
                collective_id=0, has_side_effects=True, vmem_limit_bytes=56 * 1024 * 1024
            ),
        )(phase, solute, labels, quat_table.T, heat_map, cotangent)
        final, sens = pl.pallas_call(
            store,
            out_shape=(
                jax.ShapeDtypeStruct((6, depth, rows, cols), F32),
                jax.ShapeDtypeStruct((rows, cols), F32),
            ),
            in_specs=[vmem, vmem],
            out_specs=(hbm, hbm),
            scratch_shapes=[dma(7)],
            compiler_params=pltpu.CompilerParams(vmem_limit_bytes=4 * 1024 * 1024),
        )(final, sens)
        return final, sens, obj[0, 0]

    return jax.shard_map(
        on_device,
        mesh=mesh,
        in_specs=(
            P("gz", "gy", None),
            P("gz", "gy", None),
            P("gz", "gy", None),
            P(),
            P("gy", None),
            P(None, "gz", "gy", None),
        ),
        out_specs=(P(None, "gz", "gy", None), P("gy", None), P()),
        check_vma=False,
    )
```
